256 devices in a mesh: tm: 16 (over x_hi, z), inner: 16 (over y, x_lo, core).
Axes of the slice: x: 4 (x_hi: 2, x_lo: 2; x = x_hi * 2 + x_lo), y: 4, z: 8, core: 2. Of those that a mesh axis runs over, the one named last changes fastest.
Arguments:
- start_panels: float32 [16, 192, 2048], P('tm', None, 'inner'), may hold values from -6 to 6
- kinetic: float32 [2048, 2048], P('inner')
- fields: int32 [16, 2048], P('tm'), may hold values from -1 to 1, as said below
Outputs:
- orbitals: float32 [16, 8, 192, 2048], P('tm', None, None, 'inner')
- log_scales: float32 [16, 8, 192], P('tm')
The draws below stay inside these ranges and needn't reach their ends.
Inputs may be any that keep to these rules, and one draw needn't show every extreme that they name: `fields`: each entry is -1 or +1.
All inputs are finite; a program needn't handle non-finite values.
Results may differ from the reference program's by a relative error of at most 0.0003.
Values sent between devices are 32-bit elements; how exact they have to be, the bound alone decides.
No kernel may reach another device: no remote copies, remote signals or barrier semaphores. Data moves between devices by JAX's collectives and lax.ppermute only.
A program may use at most 128 MiB of HBM per device.

```python
import math
import jax
import jax.numpy as jnp
from jax import lax

N = 2048
R = 192
L_DEV = 1
SLICES = 16
HOPS = 8
N_TM = 16


def draw_kinetic(key, part):
    noise = jnp.clip(jax.random.normal(key, (N, N), jnp.float32), -4.0, 4.0)
    return jnp.eye(N, dtype=jnp.float32) + 0.2 / math.sqrt(N) * noise


def draw_fields(key, part):
    return 2 * jax.random.randint(key, (SLICES, N), 0, 2, dtype=jnp.int32) - 1


def levels(stream_key, extent, cuts, smallest, high):
    gain, own = 1.0, jax.random.fold_in(stream_key, 6)
    for dim, parts in cuts:
        draws = jnp.exp(jax.random.uniform(jax.random.fold_in(own, dim), (parts,), jnp.float32, smallest / len(cuts), high / len(cuts)))
        gain = gain * jnp.repeat(draws, extent[dim] // parts).reshape([-1 if axis == dim else 1 for axis in range(len(extent))])
    return gain


def centred(own_key, dims, spread, bound, shards=(), kind=jnp.bfloat16):
    result = spread * jax.random.normal(own_key, dims, jnp.float32)
    if shards:
        result = result * levels(own_key, dims, shards, -0.22, 0.18)
    return jnp.clip(result, -bound, bound).astype(kind)


def setup_inputs(seed: int = 0) -> dict:
    keys = jax.random.split(jax.random.key(seed), 4)
    return {
        "start_panels": centred(keys[0], (N_TM, R, N), 1.0, 6.0, ((0, 16), (2, 16)), jnp.float32),
        "kinetic": draw_kinetic(jax.random.fold_in(keys[3], 71), 0),
        "fields": draw_fields(jax.random.fold_in(keys[3], 71), 0),
    }


coupling = 0.17725

def reference(start_panels, kinetic, fields):
    highest = lax.Precision.HIGHEST
    scales = jnp.exp(coupling * fields.astype(jnp.float32)).reshape(N_TM, L_DEV, N)
    state = start_panels
    orbit_list = []
    log_list = []
    for hop in range(HOPS):
        for layer in range(L_DEV):
            state = jnp.einsum('gcj,ij->gci', state, kinetic, precision=highest) * scales[:, layer][:, None, :]
        gram_matrix = jnp.einsum('gcj,gdj->gcd', state, state, precision=highest)
        lower = jnp.linalg.cholesky(gram_matrix)
        orthonormal = lax.linalg.triangular_solve(lower, state, left_side=True, lower=True)
        orbit_list.append(math.sqrt(N) * orthonormal)
        log_list.append(jnp.log(jnp.diagonal(lower, axis1=1, axis2=2)))
        state = jnp.roll(orthonormal, 1, axis=0)
    return (jnp.stack(orbit_list, axis=1), jnp.stack(log_list, axis=1))
```

```python
import math

import jax
import jax.numpy as jnp
from jax import lax
from jax.experimental import pallas as pl
from jax.experimental.pallas import tpu as pltpu
from jax.sharding import PartitionSpec as P

coupling = 0.17725
F32 = jnp.float32
BF16 = jnp.bfloat16
LANES = 128
PIVOTS = 8
BLOCK = 64
CHUNK = 256


def from_behind(block, axis, distance):
    devices = range(lax.axis_size(axis))
    route = [((i - distance) % len(devices), i) for i in devices]
    return lax.ppermute(block, axis, route)


def halves(value):
    high = value.astype(BF16)
    return high, (value - high.astype(F32)).astype(BF16)


def last_with_last(left, right):
    return lax.dot_general(left, right, (((1,), (1,)), ((), ())), preferred_element_type=F32)


def last_with_first(left, right):
    return lax.dot_general(left, right, (((1,), (0,)), ((), ())), preferred_element_type=F32)


def factor(gram_ref, inverse_ref, pivot_ref, beside):
    size = gram_ref.shape[0]
    lane = lax.broadcasted_iota(jnp.int32, (size, LANES), 1)
    row = lax.broadcasted_iota(jnp.int32, (size, LANES), 0)
    sublane = lax.broadcasted_iota(jnp.int32, (PIVOTS, LANES), 0)
    cut = size - LANES
    second = jnp.where(row - LANES == lane - cut, 1.0, 0.0)
    tiles = [
        gram_ref[:, :LANES],
        jnp.where(lane < cut, gram_ref[:, LANES:], second),
        jnp.where(row == lane, 1.0, 0.0),
    ]
    step = 0
    for first in range(0, size, BLOCK):
        last = first + BLOCK
        live = [t for t in range(3) if t > 0 or first < LANES]
        part = {t: tiles[t][:BLOCK] for t in live}
        done = {t: [] for t in live}
        for top in range(0, BLOCK, PIVOTS):
            column = first + top
            source = part[column // LANES]
            height = BLOCK - top
            start = column % LANES
            columns = [
                jnp.broadcast_to(source[:, start + j : start + j + 1], (height, LANES))
                for j in range(PIVOTS)
            ]
            pivots = jnp.zeros((PIVOTS, LANES), F32)
            for j in range(PIVOTS):
                pivots = jnp.where(sublane == j, columns[j][:PIVOTS], pivots)
                scaled = columns[j] * (1.0 / columns[j][j : j + 1, :])
                below = jnp.where(sublane > j, scaled[:PIVOTS], 0.0)
                if height > PIVOTS:
                    below = jnp.concatenate([below, scaled[PIVOTS:]], 0)
                for k in range(j + 1, PIVOTS):
                    columns[k] = columns[k] - below * columns[k][j : j + 1, :]
                for t in live:
                    part[t] = part[t] - below * part[t][j : j + 1, :]
            root = lax.rsqrt(pivots)
            root = root * (1.5 - 0.5 * pivots * root * root)
            pivot_ref[column : column + PIVOTS, :] = pivots
            for t in live:
                done[t].append(part[t][:PIVOTS] * root)
                part[t] = part[t][PIVOTS:]
            beside(step)
            step += 1
        full = {t: jnp.concatenate(done[t], 0) for t in live}
        inverse_ref[first:last, :LANES] = full[2]
        padding = jnp.zeros((BLOCK, LANES - cut), F32)
        corner = full[1][:, cut:] if first >= LANES else jnp.zeros((BLOCK, cut), F32)
        inverse_ref[first:last, LANES:] = jnp.concatenate([corner, padding], 1)
        if last == size:
            break
        if last < LANES:
            left = jnp.concatenate([full[0][:, last:], full[1][:, :cut]], 1)
        else:
            left = full[1][:, last - LANES : cut]
        live = [t for t in range(3) if t > 0 or last < LANES]
        update = lax.dot_general(
            left,
            jnp.concatenate([full[t] for t in live], 1),
            (((0,), (0,)), ((), ())),
            precision=lax.Precision.HIGHEST,
            preferred_element_type=F32,
        )
        for i, t in enumerate(live):
            tiles[t] = tiles[t][BLOCK:] - update[:, LANES * i : LANES * i + LANES]
        if last >= LANES:
            tiles[0] = None


def chain_kernel(
    own_ref,
    panel_ref,
    scale_ref,
    kinetic_ref,
    out_ref,
    kinetic_high,
    kinetic_low,
    buffers,
    arrived,
    panel,
    mapped,
    inverse_pair,
    gram_ref,
    inverse_ref,
    pivot_ref,
):
    rank, sites = panel_ref.shape
    hops = scale_ref.shape[0]
    chunks = sites // CHUNK
    own = pl.multiple_of(own_ref[0] * LANES, LANES)

    def load(c):
        return pltpu.make_async_copy(
            kinetic_ref.at[pl.ds(c * CHUNK, CHUNK), :], buffers.at[c % 2], arrived.at[c % 2]
        )

    def map_chunk(source, hop, c):
        at = slice(c * CHUNK, (c + 1) * CHUNK)
        both = last_with_last(source[...], kinetic_high[at, :])
        rest = last_with_last(source[:rank, :], kinetic_low[at, :])
        return (both[:rank] + both[rank:] + rest) * scale_ref[pl.ds(hop, 1), at]

    def put(target, c, value):
        high, low = halves(value)
        target[:rank, c * CHUNK : (c + 1) * CHUNK] = high
        target[rank:, c * CHUNK : (c + 1) * CHUNK] = low

    load(0).start()
    load(1).start()
    for c in range(chunks):
        put(mapped, c, panel_ref[:, c * CHUNK : (c + 1) * CHUNK])
    for c in range(chunks):
        load(c).wait()
        high, low = halves(buffers[c % 2])
        kinetic_high[c * CHUNK : (c + 1) * CHUNK, :] = high
        kinetic_low[c * CHUNK : (c + 1) * CHUNK, :] = low
        if c + 2 < chunks:
            load(c + 2).start()
        put(panel, c, map_chunk(mapped, 0, c))

    row = lax.broadcasted_iota(jnp.int32, (LANES, LANES), 0)
    lane = lax.broadcasted_iota(jnp.int32, (LANES, LANES), 1)
    diagonal = row == lane
    steps = rank // PIVOTS

    def hop_body(hop, beside):
        both = panel[...]
        products = last_with_last(both, both)
        gram = (products[:rank, :rank] + products[rank:, rank:]) + (
            products[:rank, rank:] + products[rank:, :rank]
        )
        gram_ref[:, :LANES] = gram[:, :LANES]
        gram_ref[:, LANES:] = jnp.concatenate(
            [gram[:, LANES:], jnp.zeros((rank, 2 * LANES - rank), F32)], 1
        )
        factor(gram_ref, inverse_ref, pivot_ref, beside)
        high, low = halves(inverse_ref[:, :rank])
        inverse_pair[:rank, :] = high
        inverse_pair[rank:, :] = low
        mine = panel[:, pl.ds(own, LANES)]
        products = last_with_first(inverse_pair[...], mine[:rank])
        rest = last_with_first(inverse_pair[:rank, :], mine[rank:])
        out_ref[hop, :rank, :] = (products[:rank] + products[rank:] + rest) * math.sqrt(sites)
        upper = jnp.sum(jnp.where(diagonal, pivot_ref[:LANES], 0.0), 0, keepdims=True)
        under = jnp.where(diagonal[: rank - LANES], pivot_ref[LANES:], 0.0)
        under = jnp.sum(under, 0, keepdims=True)
        under = jnp.where(lane[:1] < rank - LANES, under, 1.0)
        out_ref[hop, rank:, :] = jnp.concatenate(
            [0.5 * jnp.log(upper), 0.5 * jnp.log(under), jnp.zeros((6, LANES), F32)], 0
        )

    def whole_hop(hop, carry):
        def beside(step):
            if step % 2 == 1 and step // 2 < chunks:
                put(mapped, step // 2, map_chunk(panel, hop + 1, step // 2))

        hop_body(hop, beside)
        for c in range(chunks):
            at = slice(c * CHUNK, (c + 1) * CHUNK)
            products = last_with_first(inverse_pair[...], mapped[:rank, at])
            rest = last_with_first(inverse_pair[:rank, :], mapped[rank:, at])
            put(panel, c, products[:rank] + products[rank:] + rest)
        return carry

    lax.fori_loop(0, hops - 1, whole_hop, 0)
    hop_body(hops - 1, lambda step: None)


def run_chain(own, panel, scales, kinetic):
    rank, sites = panel.shape
    hops = scales.shape[0]
    return pl.pallas_call(
        chain_kernel,
        out_shape=jax.ShapeDtypeStruct((hops, rank + 8, LANES), F32),
        in_specs=[
            pl.BlockSpec(memory_space=pltpu.SMEM),
            pl.BlockSpec(memory_space=pltpu.VMEM),
            pl.BlockSpec(memory_space=pltpu.VMEM),
            pl.BlockSpec(memory_space=pl.ANY),
        ],
        out_specs=pl.BlockSpec(memory_space=pltpu.VMEM),
        scratch_shapes=[
            pltpu.VMEM((sites, sites), BF16),
            pltpu.VMEM((sites, sites), BF16),
            pltpu.VMEM((2, CHUNK, sites), F32),
            pltpu.SemaphoreType.DMA((2,)),
            pltpu.VMEM((2 * rank, sites), BF16),
            pltpu.VMEM((2 * rank, sites), BF16),
            pltpu.VMEM((2 * rank, rank), BF16),
            pltpu.VMEM((rank, 2 * LANES), F32),
            pltpu.VMEM((rank, 2 * LANES), F32),
            pltpu.VMEM((rank, LANES), F32),
        ],
        compiler_params=pltpu.CompilerParams(vmem_limit_bytes=48 << 20),
        name="chain",
    )(own, panel, scales, kinetic)


def on_device(start_panels, kinetic, fields):
    rank = start_panels.shape[1]
    hops = lax.axis_size("tm") // 2
    away = hops - 1
    scales = jnp.exp(coupling * fields.astype(F32))
    distance = 1
    while distance < hops:
        scales = jnp.concatenate([from_behind(scales, "tm", distance), scales], 0)
        distance *= 2
    panel = from_behind(start_panels[0], "tm", away)
    panel = lax.all_gather(panel, "inner", axis=1, tiled=True)
    whole = lax.all_gather(kinetic, "inner", axis=0, tiled=True)
    own = lax.axis_index("inner").astype(jnp.int32)[None]
    blocks = run_chain(own, panel, scales, whole)
    parts = [from_behind(blocks[k], "tm", k - away) if k < away else blocks[k] for k in range(hops)]
    orbitals = jnp.stack([part[:rank] for part in parts], 0)[None]
    logs = jnp.stack([part[rank : rank + 2].reshape(-1)[:rank] for part in parts], 0)[None]
    return (orbitals, logs)


def solution(mesh):
    placed = (P("tm", None, "inner"), P("inner", None), P("tm", None))
    return jax.shard_map(
        on_device,
        mesh=mesh,
        in_specs=placed,
        out_specs=(P("tm", None, None, "inner"), P("tm", None, None)),
        check_vma=False,
    )
```

```python
import math

import jax
import jax.numpy as jnp
from jax import lax
from jax.experimental import pallas as pl
from jax.experimental.pallas import tpu as pltpu
from jax.sharding import PartitionSpec as P

coupling = 0.17725
F32 = jnp.float32
BF16 = jnp.bfloat16
LANES = 128
PIVOTS = 8
BLOCK = 64
CHUNK = 256


Y_CHIPS = 4
X_CHIPS = 4
CORES = 2


def device(tm_size, x, y, z, core):
    z_chips = 2 * tm_size // X_CHIPS
    x, y, z = x % X_CHIPS, y % Y_CHIPS, z % z_chips
    return (x // 2 * z_chips + z, (y * 2 + x % 2) * CORES + core % CORES)


def route(block, target):
    tm_size, inner_size = lax.axis_size("tm"), lax.axis_size("inner")
    pairs = []
    for x in range(X_CHIPS):
        for y in range(Y_CHIPS):
            for z in range(2 * tm_size // X_CHIPS):
                for core in range(CORES):
                    source = device(tm_size, x, y, z, core)
                    sink = device(tm_size, *target(x, y, z, core))
                    pairs.append(tuple(tm * inner_size + i for tm, i in (source, sink)))
    return lax.ppermute(block, ("tm", "inner"), pairs)


def along_x(block, by):
    return route(block, lambda x, y, z, core: (x + by, y, z, core))


def along_y(block, by):
    return route(block, lambda x, y, z, core: (x, y + by, z, core))


def along_y_by_parity(block, by):
    return route(block, lambda x, y, z, core: (x, y + (by if z % 2 == 0 else -by), z, core))


def along_z(block, by):
    return route(block, lambda x, y, z, core: (x, y, z + by, core))


def other_core(block):
    return route(block, lambda x, y, z, core: (x, y, z, core + 1))


def from_behind(block, distance):
    tm_size = lax.axis_size("tm")
    return lax.ppermute(block, "tm", [((i - distance) % tm_size, i) for i in range(tm_size)])


def halves(value):
    high = value.astype(BF16)
    return high, (value - high.astype(F32)).astype(BF16)


def last_with_last(left, right):
    return lax.dot_general(left, right, (((1,), (1,)), ((), ())), preferred_element_type=F32)


def last_with_first(left, right):
    return lax.dot_general(left, right, (((1,), (0,)), ((), ())), preferred_element_type=F32)


def factor(gram_ref, inverse_ref, pivot_ref, beside):
    size = gram_ref.shape[0]
    lane = lax.broadcasted_iota(jnp.int32, (size, LANES), 1)
    row = lax.broadcasted_iota(jnp.int32, (size, LANES), 0)
    sublane = lax.broadcasted_iota(jnp.int32, (PIVOTS, LANES), 0)
    cut = size - LANES
    second = jnp.where(row - LANES == lane - cut, 1.0, 0.0)
    tiles = [
        gram_ref[:, :LANES],
        jnp.where(lane < cut, gram_ref[:, LANES:], second),
        jnp.where(row == lane, 1.0, 0.0),
    ]
    step = 0
    for first in range(0, size, BLOCK):
        last = first + BLOCK
        live = [t for t in range(3) if t > 0 or first < LANES]
        part = {t: tiles[t][:BLOCK] for t in live}
        done = {t: [] for t in live}
        for top in range(0, BLOCK, PIVOTS):
            column = first + top
            source = part[column // LANES]
            height = BLOCK - top
            start = column % LANES
            columns = [
                jnp.broadcast_to(source[:, start + j : start + j + 1], (height, LANES))
                for j in range(PIVOTS)
            ]
            pivots = jnp.zeros((PIVOTS, LANES), F32)
            for j in range(PIVOTS):
                pivots = jnp.where(sublane == j, columns[j][:PIVOTS], pivots)
                scaled = columns[j] * (1.0 / columns[j][j : j + 1, :])
                below = jnp.where(sublane > j, scaled[:PIVOTS], 0.0)
                if height > PIVOTS:
                    below = jnp.concatenate([below, scaled[PIVOTS:]], 0)
                for k in range(j + 1, PIVOTS):
                    columns[k] = columns[k] - below * columns[k][j : j + 1, :]
                for t in live:
                    part[t] = part[t] - below * part[t][j : j + 1, :]
            root = lax.rsqrt(pivots)
            root = root * (1.5 - 0.5 * pivots * root * root)
            pivot_ref[column : column + PIVOTS, :] = pivots
            for t in live:
                done[t].append(part[t][:PIVOTS] * root)
                part[t] = part[t][PIVOTS:]
            beside(step)
            step += 1
        full = {t: jnp.concatenate(done[t], 0) for t in live}
        inverse_ref[first:last, :LANES] = full[2]
        padding = jnp.zeros((BLOCK, LANES - cut), F32)
        corner = full[1][:, cut:] if first >= LANES else jnp.zeros((BLOCK, cut), F32)
        inverse_ref[first:last, LANES:] = jnp.concatenate([corner, padding], 1)
        if last == size:
            break
        if last < LANES:
            left = jnp.concatenate([full[0][:, last:], full[1][:, :cut]], 1)
        else:
            left = full[1][:, last - LANES : cut]
        live = [t for t in range(3) if t > 0 or last < LANES]
        update = lax.dot_general(
            left,
            jnp.concatenate([full[t] for t in live], 1),
            (((0,), (0,)), ((), ())),
            precision=lax.Precision.HIGHEST,
            preferred_element_type=F32,
        )
        for i, t in enumerate(live):
            tiles[t] = tiles[t][BLOCK:] - update[:, LANES * i : LANES * i + LANES]
        if last >= LANES:
            tiles[0] = None


def map_chunk(panel, kinetic_high, kinetic_low, scale, c):
    rank = panel.shape[0] // 2
    at = slice(c * CHUNK, (c + 1) * CHUNK)
    both = last_with_last(panel[...], kinetic_high[at, :])
    rest = last_with_last(panel[:rank, :], kinetic_low[at, :])
    return (both[:rank] + both[rank:] + rest) * scale


def put(target, at, value):
    rank = target.shape[0] // 2
    high, low = halves(value)
    target[:rank, at] = high
    target[rank:, at] = low


def normalise(own, panel, out_ref, inverse_pair, scratch, beside):
    gram_ref, inverse_ref, pivot_ref = scratch
    rank, sites = panel.shape[0] // 2, panel.shape[1]
    both = panel[...]
    products = last_with_last(both, both)
    gram = (products[:rank, :rank] + products[rank:, rank:]) + (
        products[:rank, rank:] + products[rank:, :rank]
    )
    gram_ref[:, :LANES] = gram[:, :LANES]
    gram_ref[:, LANES:] = jnp.concatenate(
        [gram[:, LANES:], jnp.zeros((rank, 2 * LANES - rank), F32)], 1
    )
    factor(gram_ref, inverse_ref, pivot_ref, beside)
    high, low = halves(inverse_ref[:, :rank])
    inverse_pair[:rank, :] = high
    inverse_pair[rank:, :] = low
    mine = panel[:, pl.ds(own, LANES)]
    products = last_with_first(inverse_pair[...], mine[:rank])
    rest = last_with_first(inverse_pair[:rank, :], mine[rank:])
    diagonal = lax.broadcasted_iota(jnp.int32, (LANES, LANES), 0) == lax.broadcasted_iota(
        jnp.int32, (LANES, LANES), 1
    )
    lane = lax.broadcasted_iota(jnp.int32, (1, LANES), 1)
    upper = jnp.sum(jnp.where(diagonal, pivot_ref[:LANES], 0.0), 0, keepdims=True)
    under = jnp.where(diagonal[: rank - LANES], pivot_ref[LANES:], 0.0)
    under = jnp.where(lane < rank - LANES, jnp.sum(under, 0, keepdims=True), 1.0)
    out_ref[:rank, :] = (products[:rank] + products[rank:] + rest) * math.sqrt(sites)
    out_ref[rank:, :] = jnp.concatenate(
        [0.5 * jnp.log(upper), 0.5 * jnp.log(under), jnp.zeros((6, LANES), F32)], 0
    )


def small_scratch(rank):
    return [
        pltpu.VMEM((rank, 2 * LANES), F32),
        pltpu.VMEM((rank, 2 * LANES), F32),
        pltpu.VMEM((rank, LANES), F32),
    ]


def spread(spots, core_spot, c, size):
    return pl.ds(pl.multiple_of(spots[core_spot] + c * size, size), size)


def load_kernel(pieces):
    def kernel(spots, near, far, *refs):
        kinetic = refs[:pieces]
        mapped, scale_ref, high_ref, low_ref, staging, arrived, panel = refs[pieces:]
        rank, sites = panel.shape[0] // 2, panel.shape[1]
        copies = []
        start = 0
        for p in range(pieces):
            size = kinetic[p].shape[0]
            copies.append(
                pltpu.make_async_copy(kinetic[p], staging.at[start : start + size, :], arrived.at[p])
            )
            copies[p].start()
            start += size
        blocks = near.shape[0]
        for q in range(2 * blocks):
            source = near if q < blocks else far
            at = pl.multiple_of(spots[3 + q], LANES)
            put(panel, pl.ds(at, LANES), source[q % blocks, :rank, :])
            hop = spots[3 + 2 * blocks + q]
            for r in range(sites // LANES):
                lanes = (r % CORES * (sites // LANES // CORES) + r // CORES) * LANES
                scale_ref[hop, :, lanes : lanes + LANES] = source[
                    q % blocks, rank + r : rank + r + 1, :
                ]
        start = 0
        for p in range(pieces):
            size = kinetic[p].shape[0]
            copies[p].wait()
            at = pl.multiple_of(spots[3 + 4 * blocks + p], size)
            for r in range(sites // LANES):
                lanes = (r % CORES * (sites // LANES // CORES) + r // CORES) * LANES
                high, low = halves(
                    staging[start : start + size, r * LANES : (r + 1) * LANES]
                )
                high_ref[pl.ds(at, size), lanes : lanes + LANES] = high
                low_ref[pl.ds(at, size), lanes : lanes + LANES] = low
            start += size
        for c in range(mapped.shape[1] // CHUNK):
            scale = scale_ref[0, :, spread(spots, 1, c, CHUNK)]
            mapped[:, c * CHUNK : (c + 1) * CHUNK] = map_chunk(panel, high_ref, low_ref, scale, c)

    return kernel


def run_load(hops, spots, near, far, kinetic):
    sites = kinetic[0].shape[1]
    rank = near.shape[1] - sites // LANES
    rows = sites // CORES
    vmem = pl.BlockSpec(memory_space=pltpu.VMEM)
    anywhere = pl.BlockSpec(memory_space=pl.ANY)
    return pl.pallas_call(
        load_kernel(len(kinetic)),
        out_shape=(
            jax.ShapeDtypeStruct((rank, rows), F32),
            jax.ShapeDtypeStruct((hops, 1, sites), F32),
            jax.ShapeDtypeStruct((rows, sites), BF16),
            jax.ShapeDtypeStruct((rows, sites), BF16),
        ),
        in_specs=[pl.BlockSpec(memory_space=pltpu.SMEM), vmem, vmem] + [anywhere] * len(kinetic),
        out_specs=(vmem, vmem, vmem, vmem),
        scratch_shapes=[
            pltpu.VMEM((rows, sites), F32),
            pltpu.SemaphoreType.DMA((len(kinetic),)),
            pltpu.VMEM((2 * rank, sites), BF16),
        ],
        compiler_params=pltpu.CompilerParams(vmem_limit_bytes=30 << 20),
        cost_estimate=pl.CostEstimate(
            flops=6 * rank * rows * sites, bytes_accessed=4 * rows * sites, transcendentals=0
        ),
        name="load",
    )(spots, near, far, *kinetic)


def hop_kernel(hop, hops, waits):
    first, last = hop == 0, hop == hops - 1

    def kernel(spots, mine, other, *refs):
        refs = refs[waits:]
        if not first:
            inverse_in, refs = refs[0], refs[1:]
        if not last:
            scale_ref, high_ref, low_ref, refs = refs[0], refs[1], refs[2], refs[3:]
        out_ref, refs = refs[0], refs[1:]
        if not last:
            inverse_pair, mapped, refs = refs[0], refs[1], refs[2:]
        panel, refs = refs[0], refs[1:]
        if last:
            inverse_pair, refs = refs[0], refs[1:]
        rank, sites = panel.shape[0] // 2, panel.shape[1]
        chunks = mine.shape[1] // CHUNK
        for c in range(chunks):
            at = slice(c * CHUNK, (c + 1) * CHUNK)
            for half, source in ((1, mine), (2, other)):
                value = source[:, at]
                if not first:
                    high, low = halves(value)
                    products = last_with_first(inverse_in[...], high)
                    rest = last_with_first(inverse_in[:rank, :], low)
                    value = products[:rank] + products[rank:] + rest
                put(panel, spread(spots, half, c, CHUNK), value)

        def beside(step):
            if not last and step % 4 == 1 and step // 4 < chunks:
                c = step // 4
                scale = scale_ref[hop + 1, :, spread(spots, 1, c, CHUNK)]
                value = map_chunk(panel, high_ref, low_ref, scale, c)
                mapped[:, c * CHUNK : (c + 1) * CHUNK] = value

        own = pl.multiple_of(spots[0], LANES)
        normalise(own, panel, out_ref, inverse_pair, refs, beside)

    return kernel


def run_hop(hop, hops, spots, mine, other, inverse, scales, high, low, waits):
    rank, rows = mine.shape
    sites = rows * CORES
    last = hop == hops - 1
    vmem = pl.BlockSpec(memory_space=pltpu.VMEM)
    operands = [inverse] if hop else []
    operands += [] if last else [scales, high, low]
    shapes = [jax.ShapeDtypeStruct((rank + 8, LANES), F32)]
    pair = (2 * rank, rank)
    if not last:
        shapes += [jax.ShapeDtypeStruct(pair, BF16), jax.ShapeDtypeStruct((rank, rows), F32)]
    return pl.pallas_call(
        hop_kernel(hop, hops, len(waits)),
        out_shape=shapes,
        in_specs=[pl.BlockSpec(memory_space=pltpu.SMEM), vmem, vmem]
        + [pl.BlockSpec(memory_space=pl.ANY)] * len(waits)
        + [vmem] * len(operands),
        out_specs=[vmem] * len(shapes),
        scratch_shapes=[pltpu.VMEM((2 * rank, sites), BF16)]
        + ([pltpu.VMEM(pair, BF16)] if last else [])
        + small_scratch(rank),
        compiler_params=pltpu.CompilerParams(vmem_limit_bytes=24 << 20),
        cost_estimate=pl.CostEstimate(
            flops=12 * rank * sites * sites, bytes_accessed=4 * rank * sites, transcendentals=0
        ),
        name="hop_" + str(hop),
    )(spots, mine, other, *waits, *operands)


def after(block, earlier):
    return block + 0.0 * earlier[:1, :1]


def gather(kinetic, panel):
    half = kinetic.shape[0] // 2
    top, bottom = kinetic[:half], kinetic[half:]
    down, up = along_y_by_parity(top, 1), along_y_by_parity(bottom, -1)
    across, back = along_x(top, 1), along_x(bottom, -1)
    panel = after(after(panel, down), up)
    swapped = route(panel, lambda x, y, z, core: (x ^ 1, y, z, core))
    far_top, far_bottom = along_y_by_parity(down, 1), along_y_by_parity(up, -1)
    x_down_top, x_up_bottom = along_x(down, 1), along_x(up, -1)
    up_top, down_bottom = along_z(down, 1), along_z(up, -1)
    pair = jnp.stack([panel, swapped], 0)
    around = [along_y(pair, 1), along_y(pair, -1), along_y(pair, 2)]
    near = jnp.concatenate([pair] + around, 0)
    far = other_core(near)
    x_far_top, x_far_bottom = along_x(far_top, 1), along_x(far_bottom, -1)
    x_up_top, x_down_bottom = along_z(x_down_top, 1), along_z(x_up_bottom, -1)
    pieces = [
        (kinetic, 0, 0, 0),
        (down, -1, 0, 0),
        (up, 1, 0, 1),
        (across, 0, 1, 0),
        (back, 0, 1, 1),
        (up_top, 1, 0, 0),
        (down_bottom, -1, 0, 1),
        (far_top, 2, 0, 0),
        (far_bottom, 2, 0, 1),
        (x_down_top, -1, 1, 0),
        (x_up_bottom, 1, 1, 1),
        (x_up_top, 1, 1, 0),
        (x_down_bottom, -1, 1, 1),
        (x_far_top, 2, 1, 0),
        (x_far_bottom, 2, 1, 1),
    ]
    return pieces, near, far, [(dy, dx) for dy in (0, -1, 1, 2) for dx in (0, 1)]


def on_device(start_panels, kinetic, fields):
    rank = start_panels.shape[1]
    rows, sites = kinetic.shape
    tm_size, inner_size = lax.axis_size("tm"), lax.axis_size("inner")
    hops = tm_size // 2
    away = hops - 1
    inner = lax.axis_index("inner").astype(jnp.int32)
    z = lax.rem(lax.axis_index("tm").astype(jnp.int32), 2 * tm_size // X_CHIPS)
    y, xl, core = inner // (2 * CORES), inner // CORES % 2, inner % CORES
    sign = 1 - 2 * (z % 2)

    def pair_index(dy, dx):
        return (y + dy) % Y_CHIPS * 2 + (xl ^ dx)

    pairs = [
        ((t - away + i % hops) % tm_size * inner_size + i, t * inner_size + i)
        for t in range(tm_size)
        for i in range(inner_size)
    ]
    scales = jnp.exp(coupling * fields.astype(F32)).reshape(sites // LANES, LANES)
    scales = lax.ppermute(scales, ("tm", "inner"), pairs)
    block = jnp.concatenate([from_behind(start_panels[0], away), scales], 0)
    pieces, near, far, offsets = gather(kinetic, block)
    chips = inner_size // CORES
    spots = [
        (core * chips + pair_index(0, 0)) * LANES,
        core * (sites // CORES),
        (1 - core) * (sites // CORES),
    ]
    blocks = [(c, pair_index(dy, dx)) for c in (core, 1 - core) for dy, dx in offsets]
    spots += [(c * chips + pair) * LANES for c, pair in blocks]
    spots += [(pair * CORES + c) % hops for c, pair in blocks]
    spots += [pair_index(dy * sign, dx) * rows + part * rows // 2 for _, dy, dx, part in pieces]
    spots = jnp.stack(spots)
    mapped, scales, high, low = run_load(hops, spots, near, far, [piece[0] for piece in pieces])
    inverse = None
    parts = []
    for hop in range(hops):
        other = other_core(mapped)
        waits = parts[hop - 2 : hop - 1] if hop >= 2 else []
        out, *state = run_hop(hop, hops, spots, mapped, other, inverse, scales, high, low, waits)
        if hop < away:
            inverse, mapped = state
            out = from_behind(out, hop - away)
        parts.append(out)
    orbitals = jnp.stack([part[:rank] for part in parts], 0)[None]
    logs = jnp.stack([part[rank : rank + 2].reshape(-1)[:rank] for part in parts], 0)[None]
    return (orbitals, logs)


def solution(mesh):
    placed = (P("tm", None, "inner"), P("inner", None), P("tm", None))
    return jax.shard_map(
        on_device,
        mesh=mesh,
        in_specs=placed,
        out_specs=(P("tm", None, None, "inner"), P("tm", None, None)),
        check_vma=False,
    )
```

```python
import functools
import math

import jax
import jax.numpy as jnp
from jax import lax
from jax.experimental import pallas as pl
from jax.experimental.pallas import tpu as pltpu
from jax.sharding import PartitionSpec as P

coupling = 0.17725
F32 = jnp.float32
BF16 = jnp.bfloat16
LANES = 128
PIVOTS = 8
BLOCK = 64
CHUNK = 256


Y_CHIPS = 4
X_CHIPS = 4
CORES = 2


def device(tm_size, x, y, z, core):
    z_chips = 2 * tm_size // X_CHIPS
    x, y, z = x % X_CHIPS, y % Y_CHIPS, z % z_chips
    return (x // 2 * z_chips + z, (y * 2 + x % 2) * CORES + core % CORES)


def route(block, target):
    tm_size, inner_size = lax.axis_size("tm"), lax.axis_size("inner")
    pairs = []
    for x in range(X_CHIPS):
        for y in range(Y_CHIPS):
            for z in range(2 * tm_size // X_CHIPS):
                for core in range(CORES):
                    source = device(tm_size, x, y, z, core)
                    sink = device(tm_size, *target(x, y, z, core))
                    pairs.append(tuple(tm * inner_size + i for tm, i in (source, sink)))
    return lax.ppermute(block, ("tm", "inner"), pairs)


def along_x(block, by):
    return route(block, lambda x, y, z, core: (x + by, y, z, core))


def along_y(block, by):
    return route(block, lambda x, y, z, core: (x, y + by, z, core))


def along_y_by_parity(block, by):
    return route(block, lambda x, y, z, core: (x, y + (by if z % 2 == 0 else -by), z, core))


def along_z(block, by):
    return route(block, lambda x, y, z, core: (x, y, z + by, core))


def other_core(block):
    return route(block, lambda x, y, z, core: (x, y, z, core + 1))


def from_behind(block, distance):
    tm_size = lax.axis_size("tm")
    return lax.ppermute(block, "tm", [((i - distance) % tm_size, i) for i in range(tm_size)])


def halves(value):
    high = value.astype(BF16)
    return high, (value - high.astype(F32)).astype(BF16)


def last_with_last(left, right):
    return lax.dot_general(left, right, (((1,), (1,)), ((), ())), preferred_element_type=F32)


def last_with_first(left, right):
    return lax.dot_general(left, right, (((1,), (0,)), ((), ())), preferred_element_type=F32)


def factor(gram_ref, inverse_ref, pivot_ref, beside):
    size = gram_ref.shape[0]
    lane = lax.broadcasted_iota(jnp.int32, (size, LANES), 1)
    row = lax.broadcasted_iota(jnp.int32, (size, LANES), 0)
    sublane = lax.broadcasted_iota(jnp.int32, (PIVOTS, LANES), 0)
    cut = size - LANES
    second = jnp.where(row - LANES == lane - cut, 1.0, 0.0)
    tiles = [
        gram_ref[:, :LANES],
        jnp.where(lane < cut, gram_ref[:, LANES:], second),
        jnp.where(row == lane, 1.0, 0.0),
    ]
    step = 0
    for first in range(0, size, BLOCK):
        last = first + BLOCK
        live = [t for t in range(3) if t > 0 or first < LANES]
        part = {t: tiles[t][:BLOCK] for t in live}
        done = {t: [] for t in live}
        for top in range(0, BLOCK, PIVOTS):
            column = first + top
            source = part[column // LANES]
            height = BLOCK - top
            start = column % LANES
            columns = [
                jnp.broadcast_to(source[:, start + j : start + j + 1], (height, LANES))
                for j in range(PIVOTS)
            ]
            pivots = jnp.zeros((PIVOTS, LANES), F32)
            for j in range(PIVOTS):
                pivots = jnp.where(sublane == j, columns[j][:PIVOTS], pivots)
                scaled = columns[j] * (1.0 / columns[j][j : j + 1, :])
                below = jnp.where(sublane > j, scaled[:PIVOTS], 0.0)
                if height > PIVOTS:
                    below = jnp.concatenate([below, scaled[PIVOTS:]], 0)
                for k in range(j + 1, PIVOTS):
                    columns[k] = columns[k] - below * columns[k][j : j + 1, :]
                for t in live:
                    part[t] = part[t] - below * part[t][j : j + 1, :]
            root = lax.rsqrt(pivots)
            root = root * (1.5 - 0.5 * pivots * root * root)
            pivot_ref[column : column + PIVOTS, :] = pivots
            for t in live:
                done[t].append(part[t][:PIVOTS] * root)
                part[t] = part[t][PIVOTS:]
            beside(step)
            step += 1
        full = {t: jnp.concatenate(done[t], 0) for t in live}
        inverse_ref[first:last, :LANES] = full[2]
        padding = jnp.zeros((BLOCK, LANES - cut), F32)
        corner = full[1][:, cut:] if first >= LANES else jnp.zeros((BLOCK, cut), F32)
        inverse_ref[first:last, LANES:] = jnp.concatenate([corner, padding], 1)
        if last == size:
            break
        if last < LANES:
            left = jnp.concatenate([full[0][:, last:], full[1][:, :cut]], 1)
        else:
            left = full[1][:, last - LANES : cut]
        live = [t for t in range(3) if t > 0 or last < LANES]
        update = lax.dot_general(
            left,
            jnp.concatenate([full[t] for t in live], 1),
            (((0,), (0,)), ((), ())),
            precision=lax.Precision.HIGHEST,
            preferred_element_type=F32,
        )
        for i, t in enumerate(live):
            tiles[t] = tiles[t][BLOCK:] - update[:, LANES * i : LANES * i + LANES]
        if last >= LANES:
            tiles[0] = None


def map_chunk(panel, kinetic_high, kinetic_low, scale, c):
    rank = panel.shape[0] // 2
    at = slice(c * CHUNK, (c + 1) * CHUNK)
    both = last_with_last(panel[...], kinetic_high[at, :])
    rest = last_with_last(panel[:rank, :], kinetic_low[at, :])
    return (both[:rank] + both[rank:] + rest) * scale


def put(target, at, value):
    rank = target.shape[0] // 2
    high, low = halves(value)
    target[:rank, at] = high
    target[rank:, at] = low


def fill_gram(panel, gram_ref):
    rank = panel.shape[0] // 2
    both = panel[...]
    products = last_with_last(both, both)
    gram = (products[:rank, :rank] + products[rank:, rank:]) + (
        products[:rank, rank:] + products[rank:, :rank]
    )
    gram_ref[:, :LANES] = gram[:, :LANES]
    gram_ref[:, LANES:] = jnp.concatenate(
        [gram[:, LANES:], jnp.zeros((rank, 2 * LANES - rank), F32)], 1
    )


def factor_kernel(root, gram_ref, own_ref, out_ref, inverse_pair, inverse_ref, pivot_ref):
    rank = gram_ref.shape[0]
    factor(gram_ref, inverse_ref, pivot_ref, lambda step: None)
    high, low = halves(inverse_ref[:, :rank])
    inverse_pair[:rank, :] = high
    inverse_pair[rank:, :] = low
    products = last_with_first(inverse_pair[...], own_ref[:rank])
    rest = last_with_first(inverse_pair[:rank, :], own_ref[rank:])
    diagonal = lax.broadcasted_iota(jnp.int32, (LANES, LANES), 0) == lax.broadcasted_iota(
        jnp.int32, (LANES, LANES), 1
    )
    lane = lax.broadcasted_iota(jnp.int32, (1, LANES), 1)
    upper = jnp.sum(jnp.where(diagonal, pivot_ref[:LANES], 0.0), 0, keepdims=True)
    under = jnp.where(diagonal[: rank - LANES], pivot_ref[LANES:], 0.0)
    under = jnp.where(lane < rank - LANES, jnp.sum(under, 0, keepdims=True), 1.0)
    out_ref[:rank, :] = (products[:rank] + products[rank:] + rest) * root
    out_ref[rank:, :] = jnp.concatenate(
        [0.5 * jnp.log(upper), 0.5 * jnp.log(under), jnp.zeros((6, LANES), F32)], 0
    )


def run_factor(hop, sites, gram, own):
    rank = gram.shape[0]
    vmem = pl.BlockSpec(memory_space=pltpu.VMEM)
    return pl.pallas_call(
        functools.partial(factor_kernel, math.sqrt(sites)),
        out_shape=(
            jax.ShapeDtypeStruct((rank + 8, LANES), F32),
            jax.ShapeDtypeStruct((2 * rank, rank), BF16),
        ),
        in_specs=[vmem, vmem],
        out_specs=(vmem, vmem),
        scratch_shapes=[
            pltpu.VMEM((rank, 2 * LANES), F32),
            pltpu.VMEM((rank, LANES), F32),
        ],
        compiler_params=pltpu.CompilerParams(vmem_limit_bytes=16 << 20),
        cost_estimate=pl.CostEstimate(
            flops=4 * rank * sites * sites, bytes_accessed=4 * rank * rank, transcendentals=0
        ),
        name="factor_" + str(hop),
    )(gram, own)


def spread(spots, core_spot, c, size):
    return pl.ds(pl.multiple_of(spots[core_spot] + c * size, size), size)


def load_kernel(pieces):
    def kernel(spots, blocks, *refs):
        kinetic = refs[:pieces]
        mapped, scale_ref, high_ref, low_ref, staging, arrived, panel = refs[pieces:]
        rank, sites = panel.shape[0] // 2, panel.shape[1]
        tiles = sites // LANES
        hops = scale_ref.shape[0]
        lanes = [(r % CORES * (tiles // CORES) + r // CORES) * LANES for r in range(tiles)]
        copies = []
        start = 0
        for p in range(pieces):
            size = kinetic[p].shape[0]
            copies.append(
                pltpu.make_async_copy(kinetic[p], staging.at[start : start + size, :], arrived.at[p])
            )
            copies[p].start()
            start += size
        for b in range(tiles):
            put(panel, slice(lanes[b], lanes[b] + LANES), blocks[b, :rank, :])
        for hop in range(hops):
            for r in range(tiles):
                scale_ref[hop, :, lanes[r] : lanes[r] + LANES] = blocks[
                    hop, rank + r : rank + r + 1, :
                ]
        start = 0
        for p in range(pieces):
            size = kinetic[p].shape[0]
            copies[p].wait()
            at = pl.multiple_of(spots[3 + p], size)
            for r in range(tiles):
                high, low = halves(staging[start : start + size, r * LANES : (r + 1) * LANES])
                high_ref[pl.ds(at, size), lanes[r] : lanes[r] + LANES] = high
                low_ref[pl.ds(at, size), lanes[r] : lanes[r] + LANES] = low
            start += size
        for c in range(mapped.shape[1] // CHUNK):
            scale = scale_ref[0, :, spread(spots, 1, c, CHUNK)]
            mapped[:, c * CHUNK : (c + 1) * CHUNK] = map_chunk(panel, high_ref, low_ref, scale, c)

    return kernel


def run_load(hops, spots, blocks, kinetic):
    sites = kinetic[0].shape[1]
    rank = blocks.shape[1] - sites // LANES
    rows = sites // CORES
    vmem = pl.BlockSpec(memory_space=pltpu.VMEM)
    return pl.pallas_call(
        load_kernel(len(kinetic)),
        out_shape=(
            jax.ShapeDtypeStruct((rank, rows), F32),
            jax.ShapeDtypeStruct((hops, 1, sites), F32),
            jax.ShapeDtypeStruct((rows, sites), BF16),
            jax.ShapeDtypeStruct((rows, sites), BF16),
        ),
        in_specs=[pl.BlockSpec(memory_space=pltpu.SMEM), vmem]
        + [pl.BlockSpec(memory_space=pltpu.HBM)] * len(kinetic),
        out_specs=(vmem, vmem, vmem, vmem),
        scratch_shapes=[
            pltpu.VMEM((rows, sites), F32),
            pltpu.SemaphoreType.DMA((len(kinetic),)),
            pltpu.VMEM((2 * rank, sites), BF16),
        ],
        compiler_params=pltpu.CompilerParams(vmem_limit_bytes=30 << 20),
        cost_estimate=pl.CostEstimate(
            flops=6 * rank * rows * sites, bytes_accessed=4 * rows * sites, transcendentals=0
        ),
        name="load",
    )(spots, blocks, *kinetic)


def map_kernel(hop, last):
    def kernel(spots, mine, other, *refs):
        if hop:
            inverse_in, refs = refs[0], refs[1:]
        if last:
            gram_ref, own_ref, panel = refs
        else:
            scale_ref, high_ref, low_ref, gram_ref, own_ref, mapped, panel = refs
        rank = panel.shape[0] // 2
        chunks = mine.shape[1] // CHUNK
        for c in range(chunks):
            at = slice(c * CHUNK, (c + 1) * CHUNK)
            for half, source in ((1, mine), (2, other)):
                value = source[:, at]
                if hop:
                    high, low = halves(value)
                    products = last_with_first(inverse_in[...], high)
                    rest = last_with_first(inverse_in[:rank, :], low)
                    value = products[:rank] + products[rank:] + rest
                put(panel, spread(spots, half, c, CHUNK), value)
        own_ref[...] = panel[:, pl.ds(pl.multiple_of(spots[0], LANES), LANES)]
        fill_gram(panel, gram_ref)
        if not last:
            for c in range(chunks):
                scale = scale_ref[hop + 1, :, spread(spots, 1, c, CHUNK)]
                value = map_chunk(panel, high_ref, low_ref, scale, c)
                mapped[:, c * CHUNK : (c + 1) * CHUNK] = value

    return kernel


def run_map(hop, hops, spots, mine, other, inverse, scales, high, low):
    rank, rows = mine.shape
    sites = rows * CORES
    last = hop == hops - 1
    vmem = pl.BlockSpec(memory_space=pltpu.VMEM)
    operands = [inverse] if hop else []
    operands += [] if last else [scales, high, low]
    shapes = [
        jax.ShapeDtypeStruct((rank, 2 * LANES), F32),
        jax.ShapeDtypeStruct((2 * rank, LANES), BF16),
    ]
    if not last:
        shapes += [jax.ShapeDtypeStruct((rank, rows), F32)]
    return pl.pallas_call(
        map_kernel(hop, last),
        out_shape=shapes,
        in_specs=[pl.BlockSpec(memory_space=pltpu.SMEM), vmem, vmem] + [vmem] * len(operands),
        out_specs=[vmem] * len(shapes),
        scratch_shapes=[pltpu.VMEM((2 * rank, sites), BF16)],
        compiler_params=pltpu.CompilerParams(vmem_limit_bytes=24 << 20),
        cost_estimate=pl.CostEstimate(
            flops=6 * rank * rows * sites, bytes_accessed=4 * rank * sites, transcendentals=0
        ),
        name="map_" + str(hop),
    )(spots, mine, other, *operands)


def gather_kinetic(kinetic):
    half = kinetic.shape[0] // 2
    top, bottom = kinetic[:half], kinetic[half:]
    down, up = along_y_by_parity(top, 1), along_y_by_parity(bottom, -1)
    across, back = along_x(top, 1), along_x(bottom, -1)
    far_top, far_bottom = along_y_by_parity(down, 1), along_y_by_parity(up, -1)
    x_down_top, x_up_bottom = along_x(down, 1), along_x(up, -1)
    up_top, down_bottom = along_z(down, 1), along_z(up, -1)
    x_far_top, x_far_bottom = along_x(far_top, 1), along_x(far_bottom, -1)
    x_up_top, x_down_bottom = along_z(x_down_top, 1), along_z(x_up_bottom, -1)
    return [
        (kinetic, 0, 0, 0),
        (down, -1, 0, 0),
        (up, 1, 0, 1),
        (across, 0, 1, 0),
        (back, 0, 1, 1),
        (up_top, 1, 0, 0),
        (down_bottom, -1, 0, 1),
        (far_top, 2, 0, 0),
        (far_bottom, 2, 0, 1),
        (x_down_top, -1, 1, 0),
        (x_up_bottom, 1, 1, 1),
        (x_up_top, 1, 1, 0),
        (x_down_bottom, -1, 1, 1),
        (x_far_top, 2, 1, 0),
        (x_far_bottom, 2, 1, 1),
    ]


def on_device(start_panels, kinetic, fields):
    rank = start_panels.shape[1]
    rows, sites = kinetic.shape
    tm_size, inner_size = lax.axis_size("tm"), lax.axis_size("inner")
    hops = tm_size // 2
    away = hops - 1
    inner = lax.axis_index("inner").astype(jnp.int32)
    z = lax.rem(lax.axis_index("tm").astype(jnp.int32), 2 * tm_size // X_CHIPS)
    y, xl, core = inner // (2 * CORES), inner // CORES % 2, inner % CORES
    sign = 1 - 2 * (z % 2)

    def pair_index(dy, dx):
        return (y + dy) % Y_CHIPS * 2 + (xl ^ dx)

    pairs = [
        ((t - away + i % hops) % tm_size * inner_size + i, t * inner_size + i)
        for t in range(tm_size)
        for i in range(inner_size)
    ]
    scales = jnp.exp(coupling * fields.astype(F32)).reshape(sites // LANES, LANES)
    scales = lax.ppermute(scales, ("tm", "inner"), pairs)
    block = jnp.concatenate([from_behind(start_panels[0], away), scales], 0)
    blocks = lax.all_gather(block, "inner", axis=0)
    pieces = gather_kinetic(kinetic)
    spots = [
        (core * (inner_size // CORES) + pair_index(0, 0)) * LANES,
        core * (sites // CORES),
        (1 - core) * (sites // CORES),
    ]
    spots += [pair_index(dy * sign, dx) * rows + part * rows // 2 for _, dy, dx, part in pieces]
    spots = jnp.stack(spots)
    mapped, scales, high, low = run_load(hops, spots, blocks, [piece[0] for piece in pieces])
    inverse = None
    parts = []
    for hop in range(hops):
        other = other_core(mapped)
        gram, own, *state = run_map(hop, hops, spots, mapped, other, inverse, scales, high, low)
        out, inverse = run_factor(hop, sites, gram, own)
        if hop < away:
            (mapped,) = state
            out = from_behind(out, hop - away)
        parts.append(out)
    orbitals = jnp.stack([part[:rank] for part in parts], 0)[None]
    logs = jnp.stack([part[rank : rank + 2].reshape(-1)[:rank] for part in parts], 0)[None]
    return (orbitals, logs)


def solution(mesh):
    placed = (P("tm", None, "inner"), P("inner", None), P("tm", None))
    return jax.shard_map(
        on_device,
        mesh=mesh,
        in_specs=placed,
        out_specs=(P("tm", None, None, "inner"), P("tm", None, None)),
        check_vma=False,
    )
```

```python
import functools
import math

import jax
import jax.numpy as jnp
from jax import lax
from jax.experimental import pallas as pl
from jax.experimental.pallas import tpu as pltpu
from jax.sharding import PartitionSpec as P

coupling = 0.17725
F32 = jnp.float32
BF16 = jnp.bfloat16
LANES = 128
PIVOTS = 8
BLOCK = 32
CHUNK = 256
TOGETHER = 3


Y_CHIPS = 4
X_CHIPS = 4
CORES = 2


def device(tm_size, x, y, z, core):
    z_chips = 2 * tm_size // X_CHIPS
    x, y, z = x % X_CHIPS, y % Y_CHIPS, z % z_chips
    return (x // 2 * z_chips + z, (y * 2 + x % 2) * CORES + core % CORES)


def route(block, target):
    tm_size, inner_size = lax.axis_size("tm"), lax.axis_size("inner")
    pairs = []
    for x in range(X_CHIPS):
        for y in range(Y_CHIPS):
            for z in range(2 * tm_size // X_CHIPS):
                for core in range(CORES):
                    source = device(tm_size, x, y, z, core)
                    sink = device(tm_size, *target(x, y, z, core))
                    pairs.append(tuple(tm * inner_size + i for tm, i in (source, sink)))
    return lax.ppermute(block, ("tm", "inner"), pairs)


def along_x(block, by):
    return route(block, lambda x, y, z, core: (x + by, y, z, core))


def along_y(block, by):
    return route(block, lambda x, y, z, core: (x, y + by, z, core))


def along_y_by_parity(block, by):
    return route(block, lambda x, y, z, core: (x, y + (by if z % 2 == 0 else -by), z, core))


def along_z(block, by):
    return route(block, lambda x, y, z, core: (x, y, z + by, core))


def other_core(block):
    return route(block, lambda x, y, z, core: (x, y, z, core + 1))


def from_behind(block, distance):
    tm_size = lax.axis_size("tm")
    return lax.ppermute(block, "tm", [((i - distance) % tm_size, i) for i in range(tm_size)])


def halves(value):
    high = value.astype(BF16)
    return high, (value - high.astype(F32)).astype(BF16)


def last_with_last(left, right):
    return lax.dot_general(left, right, (((1,), (1,)), ((), ())), preferred_element_type=F32)


def last_with_first(left, right):
    return lax.dot_general(left, right, (((1,), (0,)), ((), ())), preferred_element_type=F32)


def factor(gram_ref, inverse_ref, pivot_ref):
    size = gram_ref.shape[0]
    lane = lax.broadcasted_iota(jnp.int32, (size, LANES), 1)
    row = lax.broadcasted_iota(jnp.int32, (size, LANES), 0)
    sublane = lax.broadcasted_iota(jnp.int32, (PIVOTS, LANES), 0)
    cut = size - LANES
    second = jnp.where(row - LANES == lane - cut, 1.0, 0.0)
    tiles = [
        gram_ref[:, :LANES],
        jnp.where(lane < cut, gram_ref[:, LANES:], second),
        jnp.where(row == lane, 1.0, 0.0),
    ]

    def columns_at(source, column):
        start = column % LANES
        return [
            jnp.broadcast_to(source[:, start + j : start + j + 1], (source.shape[0], LANES))
            for j in range(PIVOTS)
        ]

    for first in range(0, size, BLOCK):
        last = first + BLOCK
        live = [t for t in range(3) if t > 0 or first < LANES]
        part = {t: tiles[t][:BLOCK] for t in live}
        done = {t: [] for t in live}
        columns = columns_at(part[first // LANES], first)
        for top in range(0, BLOCK, PIVOTS):
            column = first + top
            ahead = []
            if top + PIVOTS < BLOCK:
                ahead = columns_at(part[(column + PIVOTS) // LANES], column + PIVOTS)
            pivots = jnp.zeros((PIVOTS, LANES), F32)
            for j in range(PIVOTS):
                pivots = jnp.where(sublane == j, columns[j][:PIVOTS], pivots)
                scaled = columns[j] * (1.0 / columns[j][j : j + 1, :])
                below = jnp.where(sublane > j, scaled[:PIVOTS], 0.0)
                if scaled.shape[0] > PIVOTS:
                    below = jnp.concatenate([below, scaled[PIVOTS:]], 0)
                for k in range(j + 1, PIVOTS):
                    columns[k] = columns[k] - below * columns[k][j : j + 1, :]
                ahead = [later - below * later[j : j + 1, :] for later in ahead]
                for t in live:
                    part[t] = part[t] - below * part[t][j : j + 1, :]
            columns = [later[PIVOTS:] for later in ahead]
            root = lax.rsqrt(pivots)
            root = root * (1.5 - 0.5 * pivots * root * root)
            pivot_ref[column : column + PIVOTS, :] = pivots
            for t in live:
                done[t].append(part[t][:PIVOTS] * root)
                part[t] = part[t][PIVOTS:]
        full = {t: jnp.concatenate(done[t], 0) for t in live}
        inverse_ref[first:last, :LANES] = full[2]
        padding = jnp.zeros((BLOCK, LANES - cut), F32)
        corner = full[1][:, cut:] if last > LANES else jnp.zeros((BLOCK, cut), F32)
        inverse_ref[first:last, LANES:] = jnp.concatenate([corner, padding], 1)
        if last == size:
            break
        if last < LANES:
            left = jnp.concatenate([full[0][:, last:], full[1][:, :cut]], 1)
        else:
            left = full[1][:, last - LANES : cut]
        live = [t for t in range(3) if t > 0 or last < LANES]
        left_high, left_low = halves(left)
        right_high, right_low = halves(jnp.concatenate([full[t] for t in live], 1))
        update = lax.dot_general(
            jnp.concatenate([left_high, left_high, left_low, left_low], 0),
            jnp.concatenate([right_high, right_low, right_high, right_low], 0),
            (((0,), (0,)), ((), ())),
            preferred_element_type=F32,
        )
        for i, t in enumerate(live):
            tiles[t] = tiles[t][BLOCK:] - update[:, LANES * i : LANES * i + LANES]
        if last >= LANES:
            tiles[0] = None


def map_chunk(panel, kinetic_high, kinetic_low, scale, c):
    rank = panel.shape[0] // 2
    at = slice(c * CHUNK, (c + 1) * CHUNK)
    both = last_with_last(panel[...], kinetic_high[at, :])
    rest = last_with_last(panel[:rank, :], kinetic_low[at, :])
    return (both[:rank] + both[rank:] + rest) * scale


def put(target, at, value):
    rank = target.shape[0] // 2
    high, low = halves(value)
    target[:rank, at] = high
    target[rank:, at] = low


def fill_gram(panel, gram_ref):
    rank = panel.shape[0] // 2
    both = panel[...]
    products = last_with_last(both, both)
    gram = (products[:rank, :rank] + products[rank:, rank:]) + (
        products[:rank, rank:] + products[rank:, :rank]
    )
    gram_ref[:, :LANES] = gram[:, :LANES]
    gram_ref[:, LANES:] = jnp.concatenate(
        [gram[:, LANES:], jnp.zeros((rank, 2 * LANES - rank), F32)], 1
    )


def factor_kernel(root, gram_ref, own_ref, out_ref, inverse_pair, inverse_ref, pivot_ref):
    rank = gram_ref.shape[0]
    factor(gram_ref, inverse_ref, pivot_ref)
    high, low = halves(inverse_ref[:, :rank])
    inverse_pair[:rank, :] = high
    inverse_pair[rank:, :] = low
    products = last_with_first(inverse_pair[...], own_ref[:rank])
    rest = last_with_first(inverse_pair[:rank, :], own_ref[rank:])
    diagonal = lax.broadcasted_iota(jnp.int32, (LANES, LANES), 0) == lax.broadcasted_iota(
        jnp.int32, (LANES, LANES), 1
    )
    lane = lax.broadcasted_iota(jnp.int32, (1, LANES), 1)
    upper = jnp.sum(jnp.where(diagonal, pivot_ref[:LANES], 0.0), 0, keepdims=True)
    under = jnp.where(diagonal[: rank - LANES], pivot_ref[LANES:], 0.0)
    under = jnp.where(lane < rank - LANES, jnp.sum(under, 0, keepdims=True), 1.0)
    out_ref[:rank, :] = (products[:rank] + products[rank:] + rest) * root
    out_ref[rank:, :] = jnp.concatenate(
        [0.5 * jnp.log(upper), 0.5 * jnp.log(under), jnp.zeros((6, LANES), F32)], 0
    )


def run_factor(hop, sites, gram, own):
    rank = gram.shape[0]
    vmem = pl.BlockSpec(memory_space=pltpu.VMEM)
    return pl.pallas_call(
        functools.partial(factor_kernel, math.sqrt(sites)),
        out_shape=(
            jax.ShapeDtypeStruct((rank + 8, LANES), F32),
            jax.ShapeDtypeStruct((2 * rank, rank), BF16),
        ),
        in_specs=[vmem, vmem],
        out_specs=(vmem, vmem),
        scratch_shapes=[
            pltpu.VMEM((rank, 2 * LANES), F32),
            pltpu.VMEM((rank, LANES), F32),
        ],
        compiler_params=pltpu.CompilerParams(vmem_limit_bytes=16 << 20),
        cost_estimate=pl.CostEstimate(
            flops=5 * rank * sites * sites, bytes_accessed=4 * rank * rank, transcendentals=0
        ),
        name="factor_" + str(hop),
    )(gram, own)


def spread(spots, core_spot, c, size):
    return pl.ds(pl.multiple_of(spots[core_spot] + c * size, size), size)


def load_kernel(pieces):
    def kernel(spots, blocks, scales, *refs):
        kinetic = refs[:pieces]
        mapped, scale_ref, high_ref, low_ref, panel = refs[pieces:]
        tiles = panel.shape[1] // LANES
        hops = scale_ref.shape[0]
        lanes = [(r % CORES * (tiles // CORES) + r // CORES) * LANES for r in range(tiles)]
        for b in range(tiles):
            put(panel, slice(lanes[b], lanes[b] + LANES), blocks[b])
        for hop in range(hops):
            for r in range(tiles):
                scale_ref[hop, :, lanes[r] : lanes[r] + LANES] = scales[hop, r : r + 1, :]
        for p in range(pieces):
            size = kinetic[p].shape[0]
            at = pl.multiple_of(spots[3 + p], size)
            for r in range(tiles):
                high, low = halves(kinetic[p][:, r * LANES : (r + 1) * LANES])
                high_ref[pl.ds(at, size), lanes[r] : lanes[r] + LANES] = high
                low_ref[pl.ds(at, size), lanes[r] : lanes[r] + LANES] = low
        for c in range(mapped.shape[1] // CHUNK):
            scale = scale_ref[0, :, spread(spots, 1, c, CHUNK)]
            mapped[:, c * CHUNK : (c + 1) * CHUNK] = map_chunk(panel, high_ref, low_ref, scale, c)

    return kernel


def run_load(hops, spots, blocks, scales, kinetic):
    sites = kinetic[0].shape[1]
    rank = blocks.shape[1]
    rows = sites // CORES
    vmem = pl.BlockSpec(memory_space=pltpu.VMEM)
    return pl.pallas_call(
        load_kernel(len(kinetic)),
        out_shape=(
            jax.ShapeDtypeStruct((rank, rows), F32),
            jax.ShapeDtypeStruct((hops, 1, sites), F32),
            jax.ShapeDtypeStruct((rows, sites), BF16),
            jax.ShapeDtypeStruct((rows, sites), BF16),
        ),
        in_specs=[pl.BlockSpec(memory_space=pltpu.SMEM), vmem, vmem] + [vmem] * len(kinetic),
        out_specs=(vmem, vmem, vmem, vmem),
        scratch_shapes=[pltpu.VMEM((2 * rank, sites), BF16)],
        compiler_params=pltpu.CompilerParams(vmem_limit_bytes=30 << 20),
        cost_estimate=pl.CostEstimate(
            flops=6 * rank * rows * sites, bytes_accessed=4 * rows * sites, transcendentals=0
        ),
        name="load",
    )(spots, blocks, scales, *kinetic)


def map_kernel(hop, last):
    def kernel(spots, mine, other, *refs):
        if hop:
            inverse_in, refs = refs[0], refs[1:]
        if last:
            gram_ref, own_ref, panel = refs
        else:
            scale_ref, high_ref, low_ref, gram_ref, own_ref, mapped, panel = refs
        rank = panel.shape[0] // 2
        chunks = mine.shape[1] // CHUNK
        for c in range(chunks):
            at = slice(c * CHUNK, (c + 1) * CHUNK)
            for half, source in ((1, mine), (2, other)):
                value = source[:, at]
                if hop:
                    high, low = halves(value)
                    products = last_with_first(inverse_in[...], high)
                    rest = last_with_first(inverse_in[:rank, :], low)
                    value = products[:rank] + products[rank:] + rest
                put(panel, spread(spots, half, c, CHUNK), value)
        own_ref[...] = panel[:, pl.ds(pl.multiple_of(spots[0], LANES), LANES)]
        fill_gram(panel, gram_ref)
        if not last:
            for c in range(chunks):
                scale = scale_ref[hop + 1, :, spread(spots, 1, c, CHUNK)]
                value = map_chunk(panel, high_ref, low_ref, scale, c)
                mapped[:, c * CHUNK : (c + 1) * CHUNK] = value

    return kernel


def run_map(hop, hops, spots, mine, other, inverse, scales, high, low):
    rank, rows = mine.shape
    sites = rows * CORES
    last = hop == hops - 1
    vmem = pl.BlockSpec(memory_space=pltpu.VMEM)
    operands = [inverse] if hop else []
    operands += [] if last else [scales, high, low]
    shapes = [
        jax.ShapeDtypeStruct((rank, 2 * LANES), F32),
        jax.ShapeDtypeStruct((2 * rank, LANES), BF16),
    ]
    if not last:
        shapes += [jax.ShapeDtypeStruct((rank, rows), F32)]
    return pl.pallas_call(
        map_kernel(hop, last),
        out_shape=shapes,
        in_specs=[pl.BlockSpec(memory_space=pltpu.SMEM), vmem, vmem] + [vmem] * len(operands),
        out_specs=[vmem] * len(shapes),
        scratch_shapes=[pltpu.VMEM((2 * rank, sites), BF16)],
        compiler_params=pltpu.CompilerParams(vmem_limit_bytes=24 << 20),
        cost_estimate=pl.CostEstimate(
            flops=6 * rank * rows * sites, bytes_accessed=4 * rank * sites, transcendentals=0
        ),
        name="map_" + str(hop),
    )(spots, mine, other, *operands)


def gather_kinetic(kinetic):
    half = kinetic.shape[0] // 2
    top, bottom = kinetic[:half], kinetic[half:]
    down, up = along_y_by_parity(top, 1), along_y_by_parity(bottom, -1)
    across, back = along_x(top, 1), along_x(bottom, -1)
    far_top, far_bottom = along_y_by_parity(down, 1), along_y_by_parity(up, -1)
    x_down_top, x_up_bottom = along_x(down, 1), along_x(up, -1)
    up_top, down_bottom = along_z(down, 1), along_z(up, -1)
    x_far_top, x_far_bottom = along_x(far_top, 1), along_x(far_bottom, -1)
    x_up_top, x_down_bottom = along_z(x_down_top, 1), along_z(x_up_bottom, -1)
    return [
        (kinetic, 0, 0, 0),
        (down, -1, 0, 0),
        (up, 1, 0, 1),
        (across, 0, 1, 0),
        (back, 0, 1, 1),
        (up_top, 1, 0, 0),
        (down_bottom, -1, 0, 1),
        (far_top, 2, 0, 0),
        (far_bottom, 2, 0, 1),
        (x_down_top, -1, 1, 0),
        (x_up_bottom, 1, 1, 1),
        (x_up_top, 1, 1, 0),
        (x_down_bottom, -1, 1, 1),
        (x_far_top, 2, 1, 0),
        (x_far_bottom, 2, 1, 1),
    ]


def on_device(start_panels, kinetic, fields):
    rank = start_panels.shape[1]
    rows, sites = kinetic.shape
    tm_size, inner_size = lax.axis_size("tm"), lax.axis_size("inner")
    hops = tm_size // 2
    inner = lax.axis_index("inner").astype(jnp.int32)
    z = lax.rem(lax.axis_index("tm").astype(jnp.int32), 2 * tm_size // X_CHIPS)
    y, xl, core = inner // (2 * CORES), inner // CORES % 2, inner % CORES
    sign = 1 - 2 * (z % 2)

    def pair_index(dy, dx):
        return (y + dy) % Y_CHIPS * 2 + (xl ^ dx)

    pairs = [
        ((t + i % hops) % tm_size * inner_size + i, t * inner_size + i)
        for t in range(tm_size)
        for i in range(inner_size)
    ]
    blocks = lax.all_gather(start_panels[0], "inner", axis=0)
    pieces = gather_kinetic(kinetic)
    scales = jnp.exp(coupling * fields.astype(F32)).reshape(sites // LANES, LANES)
    scales = scales + 0.0 * pieces[1][0][:1, :1]
    scales = lax.ppermute(scales, ("tm", "inner"), pairs)
    scales = lax.all_gather(scales, "inner", axis=0)
    spots = [
        (core * (inner_size // CORES) + pair_index(0, 0)) * LANES,
        core * (sites // CORES),
        (1 - core) * (sites // CORES),
    ]
    spots += [pair_index(dy * sign, dx) * rows + part * rows // 2 for _, dy, dx, part in pieces]
    spots = jnp.stack(spots)
    mapped, scales, high, low = run_load(hops, spots, blocks, scales, [piece[0] for piece in pieces])
    inverse = None
    parts = []
    for hop in range(hops):
        other = other_core(mapped)
        gram, own, *state = run_map(hop, hops, spots, mapped, other, inverse, scales, high, low)
        out, inverse = run_factor(hop, sites, gram, own)
        if state:
            (mapped,) = state
        parts.append(from_behind(out, hop) if 0 < hop < hops - TOGETHER else out)
    final = parts[-1][:1, :1]
    for hop in range(hops - TOGETHER, hops):
        block = parts[hop] if hop == hops - 1 else parts[hop] + 0.0 * final
        parts[hop] = from_behind(block, hop)
    orbitals = jnp.stack([part[:rank] for part in parts], 0)[None]
    logs = jnp.stack([part[rank : rank + 2].reshape(-1)[:rank] for part in parts], 0)[None]
    return (orbitals, logs)


def solution(mesh):
    placed = (P("tm", None, "inner"), P("inner", None), P("tm", None))
    return jax.shard_map(
        on_device,
        mesh=mesh,
        in_specs=placed,
        out_specs=(P("tm", None, None, "inner"), P("tm", None, None)),
        check_vma=False,
    )
```

```python
import functools
import math

import jax
import jax.numpy as jnp
from jax import lax
from jax.experimental import pallas as pl
from jax.experimental.pallas import tpu as pltpu
from jax.sharding import PartitionSpec as P

coupling = 0.17725
F32 = jnp.float32
BF16 = jnp.bfloat16
LANES = 128
PIVOTS = 8
BLOCK = 32
CHUNK = 256
TOGETHER = 2


Y_CHIPS = 4
X_CHIPS = 4
CORES = 2


def device(tm_size, x, y, z, core):
    z_chips = 2 * tm_size // X_CHIPS
    x, y, z = x % X_CHIPS, y % Y_CHIPS, z % z_chips
    return (x // 2 * z_chips + z, (y * 2 + x % 2) * CORES + core % CORES)


def route(block, target):
    tm_size, inner_size = lax.axis_size("tm"), lax.axis_size("inner")
    pairs = []
    for x in range(X_CHIPS):
        for y in range(Y_CHIPS):
            for z in range(2 * tm_size // X_CHIPS):
                for core in range(CORES):
                    source = device(tm_size, x, y, z, core)
                    sink = device(tm_size, *target(x, y, z, core))
                    pairs.append(tuple(tm * inner_size + i for tm, i in (source, sink)))
    return lax.ppermute(block, ("tm", "inner"), pairs)


def along_x(block, by):
    return route(block, lambda x, y, z, core: (x + by, y, z, core))


def along_y(block, by):
    return route(block, lambda x, y, z, core: (x, y + by, z, core))


def along_y_by_parity(block, by):
    return route(block, lambda x, y, z, core: (x, y + (by if z % 2 == 0 else -by), z, core))


def along_z(block, by):
    return route(block, lambda x, y, z, core: (x, y, z + by, core))


def other_core(block):
    return route(block, lambda x, y, z, core: (x, y, z, core + 1))


def from_behind(block, distance):
    tm_size = lax.axis_size("tm")
    return lax.ppermute(block, "tm", [((i - distance) % tm_size, i) for i in range(tm_size)])


def halves(value):
    high = value.astype(BF16)
    return high, (value - high.astype(F32)).astype(BF16)


def last_with_last(left, right):
    return lax.dot_general(left, right, (((1,), (1,)), ((), ())), preferred_element_type=F32)


def last_with_first(left, right):
    return lax.dot_general(left, right, (((1,), (0,)), ((), ())), preferred_element_type=F32)


def factor(gram_ref, inverse_ref, pivot_ref):
    size = gram_ref.shape[0]
    lane = lax.broadcasted_iota(jnp.int32, (size, LANES), 1)
    row = lax.broadcasted_iota(jnp.int32, (size, LANES), 0)
    sublane = lax.broadcasted_iota(jnp.int32, (PIVOTS, LANES), 0)
    cut = size - LANES
    second = jnp.where(row - LANES == lane - cut, 1.0, 0.0)
    tiles = [
        gram_ref[:, :LANES],
        jnp.where(lane < cut, gram_ref[:, LANES:], second),
        jnp.where(row == lane, 1.0, 0.0),
    ]

    def columns_at(source, column):
        start = column % LANES
        return [
            jnp.broadcast_to(source[:, start + j : start + j + 1], (source.shape[0], LANES))
            for j in range(PIVOTS)
        ]

    for first in range(0, size, BLOCK):
        last = first + BLOCK
        live = [t for t in range(3) if t > 0 or first < LANES]
        part = {t: tiles[t][:BLOCK] for t in live}
        done = {t: [] for t in live}
        columns = columns_at(part[first // LANES], first)
        for top in range(0, BLOCK, PIVOTS):
            column = first + top
            ahead = []
            if top + PIVOTS < BLOCK:
                ahead = columns_at(part[(column + PIVOTS) // LANES], column + PIVOTS)
            pivots = jnp.zeros((PIVOTS, LANES), F32)
            for j in range(PIVOTS):
                pivots = jnp.where(sublane == j, columns[j][:PIVOTS], pivots)
                scaled = columns[j] * (1.0 / columns[j][j : j + 1, :])
                below = jnp.where(sublane > j, scaled[:PIVOTS], 0.0)
                if scaled.shape[0] > PIVOTS:
                    below = jnp.concatenate([below, scaled[PIVOTS:]], 0)
                for k in range(j + 1, PIVOTS):
                    columns[k] = columns[k] - below * columns[k][j : j + 1, :]
                ahead = [later - below * later[j : j + 1, :] for later in ahead]
                for t in live:
                    part[t] = part[t] - below * part[t][j : j + 1, :]
            columns = [later[PIVOTS:] for later in ahead]
            root = lax.rsqrt(pivots)
            root = root * (1.5 - 0.5 * pivots * root * root)
            pivot_ref[column : column + PIVOTS, :] = pivots
            for t in live:
                done[t].append(part[t][:PIVOTS] * root)
                part[t] = part[t][PIVOTS:]
        full = {t: jnp.concatenate(done[t], 0) for t in live}
        inverse_ref[first:last, :LANES] = full[2]
        padding = jnp.zeros((BLOCK, LANES - cut), F32)
        corner = full[1][:, cut:] if last > LANES else jnp.zeros((BLOCK, cut), F32)
        inverse_ref[first:last, LANES:] = jnp.concatenate([corner, padding], 1)
        if last == size:
            break
        if last < LANES:
            left = jnp.concatenate([full[0][:, last:], full[1][:, :cut]], 1)
        else:
            left = full[1][:, last - LANES : cut]
        live = [t for t in range(3) if t > 0 or last < LANES]
        left_high, left_low = halves(left)
        right_high, right_low = halves(jnp.concatenate([full[t] for t in live], 1))
        update = lax.dot_general(
            jnp.concatenate([left_high, left_high, left_low, left_low], 0),
            jnp.concatenate([right_high, right_low, right_high, right_low], 0),
            (((0,), (0,)), ((), ())),
            preferred_element_type=F32,
        )
        for i, t in enumerate(live):
            tiles[t] = tiles[t][BLOCK:] - update[:, LANES * i : LANES * i + LANES]
        if last >= LANES:
            tiles[0] = None


def map_chunk(panel, kinetic_high, kinetic_low, scale, c):
    rank = panel.shape[0] // 2
    at = slice(c * CHUNK, (c + 1) * CHUNK)
    both = last_with_last(panel[...], kinetic_high[at, :])
    rest = last_with_last(panel[:rank, :], kinetic_low[at, :])
    return (both[:rank] + both[rank:] + rest) * scale


def put(target, at, value):
    rank = target.shape[0] // 2
    high, low = halves(value)
    target[:rank, at] = high
    target[rank:, at] = low


def fill_gram(panel, gram_ref):
    rank = panel.shape[0] // 2
    both = panel[...]
    products = last_with_last(both, both)
    gram = (products[:rank, :rank] + products[rank:, rank:]) + (
        products[:rank, rank:] + products[rank:, :rank]
    )
    gram_ref[:, :LANES] = gram[:, :LANES]
    gram_ref[:, LANES:] = jnp.concatenate(
        [gram[:, LANES:], jnp.zeros((rank, 2 * LANES - rank), F32)], 1
    )


def factor_kernel(root, gram_ref, own_ref, out_ref, inverse_pair, inverse_ref, pivot_ref):
    rank = gram_ref.shape[0]
    factor(gram_ref, inverse_ref, pivot_ref)
    high, low = halves(inverse_ref[:, :rank])
    inverse_pair[:rank, :] = high
    inverse_pair[rank:, :] = low
    products = last_with_first(inverse_pair[...], own_ref[:rank])
    rest = last_with_first(inverse_pair[:rank, :], own_ref[rank:])
    diagonal = lax.broadcasted_iota(jnp.int32, (LANES, LANES), 0) == lax.broadcasted_iota(
        jnp.int32, (LANES, LANES), 1
    )
    lane = lax.broadcasted_iota(jnp.int32, (1, LANES), 1)
    upper = jnp.sum(jnp.where(diagonal, pivot_ref[:LANES], 0.0), 0, keepdims=True)
    under = jnp.where(diagonal[: rank - LANES], pivot_ref[LANES:], 0.0)
    under = jnp.where(lane < rank - LANES, jnp.sum(under, 0, keepdims=True), 1.0)
    out_ref[:rank, :] = (products[:rank] + products[rank:] + rest) * root
    out_ref[rank:, :] = jnp.concatenate(
        [0.5 * jnp.log(upper), 0.5 * jnp.log(under), jnp.zeros((6, LANES), F32)], 0
    )


def run_factor(hop, sites, gram, own):
    rank = gram.shape[0]
    vmem = pl.BlockSpec(memory_space=pltpu.VMEM)
    return pl.pallas_call(
        functools.partial(factor_kernel, math.sqrt(sites)),
        out_shape=(
            jax.ShapeDtypeStruct((rank + 8, LANES), F32),
            jax.ShapeDtypeStruct((2 * rank, rank), BF16),
        ),
        in_specs=[vmem, vmem],
        out_specs=(vmem, vmem),
        scratch_shapes=[
            pltpu.VMEM((rank, 2 * LANES), F32),
            pltpu.VMEM((rank, LANES), F32),
        ],
        compiler_params=pltpu.CompilerParams(vmem_limit_bytes=16 << 20),
        cost_estimate=pl.CostEstimate(
            flops=5 * rank * sites * sites, bytes_accessed=4 * rank * rank, transcendentals=0
        ),
        name="factor_" + str(hop),
    )(gram, own)


def spread(spots, core_spot, c, size):
    return pl.ds(pl.multiple_of(spots[core_spot] + c * size, size), size)


def load_kernel(pieces):
    def kernel(spots, blocks_in, *refs):
        kinetic = refs[:pieces]
        mapped, scale_ref, high_ref, low_ref, panel, blocks, own_rows, arrived = refs[pieces:]
        rank, tiles = panel.shape[0] // 2, panel.shape[1] // LANES
        hops = scale_ref.shape[0]
        lanes = [(r % CORES * (tiles // CORES) + r // CORES) * LANES for r in range(tiles)]
        copies = [
            pltpu.make_async_copy(kinetic[0], own_rows, arrived.at[0]),
            pltpu.make_async_copy(blocks_in, blocks, arrived.at[1]),
        ]
        for copy in copies:
            copy.start()
        for p in list(range(1, pieces)) + [0]:
            if p == 0:
                copies[0].wait()
            source = kinetic[p] if p else own_rows
            size = source.shape[0]
            at = pl.multiple_of(spots[3 + p], size)
            for r in range(tiles):
                high, low = halves(source[:, r * LANES : (r + 1) * LANES])
                high_ref[pl.ds(at, size), lanes[r] : lanes[r] + LANES] = high
                low_ref[pl.ds(at, size), lanes[r] : lanes[r] + LANES] = low
        copies[1].wait()
        for b in range(tiles):
            put(panel, slice(lanes[b], lanes[b] + LANES), blocks[b, :rank, :])
        for hop in range(hops):
            for r in range(tiles):
                scale_ref[hop, :, lanes[r] : lanes[r] + LANES] = blocks[
                    hop, rank + r : rank + r + 1, :
                ]
        for c in range(mapped.shape[1] // CHUNK):
            scale = scale_ref[0, :, spread(spots, 1, c, CHUNK)]
            mapped[:, c * CHUNK : (c + 1) * CHUNK] = map_chunk(panel, high_ref, low_ref, scale, c)

    return kernel


def run_load(hops, spots, blocks, kinetic):
    sites = kinetic[0].shape[1]
    rank = blocks.shape[1] - sites // LANES
    rows = sites // CORES
    vmem = pl.BlockSpec(memory_space=pltpu.VMEM)
    hbm = pl.BlockSpec(memory_space=pltpu.HBM)
    return pl.pallas_call(
        load_kernel(len(kinetic)),
        out_shape=(
            jax.ShapeDtypeStruct((rank, rows), F32),
            jax.ShapeDtypeStruct((hops, 1, sites), F32),
            jax.ShapeDtypeStruct((rows, sites), BF16),
            jax.ShapeDtypeStruct((rows, sites), BF16),
        ),
        in_specs=[pl.BlockSpec(memory_space=pltpu.SMEM), hbm, hbm]
        + [vmem] * (len(kinetic) - 1),
        out_specs=(vmem, vmem, vmem, vmem),
        scratch_shapes=[
            pltpu.VMEM((2 * rank, sites), BF16),
            pltpu.VMEM(blocks.shape, F32),
            pltpu.VMEM(kinetic[0].shape, F32),
            pltpu.SemaphoreType.DMA((2,)),
        ],
        compiler_params=pltpu.CompilerParams(vmem_limit_bytes=30 << 20),
        cost_estimate=pl.CostEstimate(
            flops=6 * rank * rows * sites, bytes_accessed=4 * rows * sites, transcendentals=0
        ),
        name="load",
    )(spots, blocks, *kinetic)


def map_kernel(hop, last):
    def kernel(spots, mine, other, *refs):
        if hop:
            inverse_in, refs = refs[0], refs[1:]
        if last:
            gram_ref, own_ref, panel = refs
        else:
            scale_ref, high_ref, low_ref, gram_ref, own_ref, mapped, panel = refs
        rank = panel.shape[0] // 2
        chunks = mine.shape[1] // CHUNK
        for c in range(chunks):
            at = slice(c * CHUNK, (c + 1) * CHUNK)
            for half, source in ((1, mine), (2, other)):
                value = source[:, at]
                if hop:
                    high, low = halves(value)
                    products = last_with_first(inverse_in[...], high)
                    rest = last_with_first(inverse_in[:rank, :], low)
                    value = products[:rank] + products[rank:] + rest
                put(panel, spread(spots, half, c, CHUNK), value)
        own_ref[...] = panel[:, pl.ds(pl.multiple_of(spots[0], LANES), LANES)]
        fill_gram(panel, gram_ref)
        if not last:
            for c in range(chunks):
                scale = scale_ref[hop + 1, :, spread(spots, 1, c, CHUNK)]
                value = map_chunk(panel, high_ref, low_ref, scale, c)
                mapped[:, c * CHUNK : (c + 1) * CHUNK] = value

    return kernel


def run_map(hop, hops, spots, mine, other, inverse, scales, high, low):
    rank, rows = mine.shape
    sites = rows * CORES
    last = hop == hops - 1
    vmem = pl.BlockSpec(memory_space=pltpu.VMEM)
    operands = [inverse] if hop else []
    operands += [] if last else [scales, high, low]
    shapes = [
        jax.ShapeDtypeStruct((rank, 2 * LANES), F32),
        jax.ShapeDtypeStruct((2 * rank, LANES), BF16),
    ]
    if not last:
        shapes += [jax.ShapeDtypeStruct((rank, rows), F32)]
    return pl.pallas_call(
        map_kernel(hop, last),
        out_shape=shapes,
        in_specs=[pl.BlockSpec(memory_space=pltpu.SMEM), vmem, vmem] + [vmem] * len(operands),
        out_specs=[vmem] * len(shapes),
        scratch_shapes=[pltpu.VMEM((2 * rank, sites), BF16)],
        compiler_params=pltpu.CompilerParams(vmem_limit_bytes=24 << 20),
        cost_estimate=pl.CostEstimate(
            flops=6 * rank * rows * sites, bytes_accessed=4 * rank * sites, transcendentals=0
        ),
        name="map_" + str(hop),
    )(spots, mine, other, *operands)


def gather_kinetic(kinetic):
    half = kinetic.shape[0] // 2
    top, bottom = kinetic[:half], kinetic[half:]
    down, up = along_y_by_parity(top, 1), along_y_by_parity(bottom, -1)
    across, back = along_x(top, 1), along_x(bottom, -1)
    far_top, far_bottom = along_y_by_parity(down, 1), along_y_by_parity(up, -1)
    x_down_top, x_up_bottom = along_x(down, 1), along_x(up, -1)
    up_top, down_bottom = along_z(down, 1), along_z(up, -1)
    x_far_top, x_far_bottom = along_x(far_top, 1), along_x(far_bottom, -1)
    x_up_top, x_down_bottom = along_z(x_down_top, 1), along_z(x_up_bottom, -1)
    return [
        (kinetic, 0, 0, 0),
        (down, -1, 0, 0),
        (up, 1, 0, 1),
        (across, 0, 1, 0),
        (back, 0, 1, 1),
        (up_top, 1, 0, 0),
        (down_bottom, -1, 0, 1),
        (far_top, 2, 0, 0),
        (far_bottom, 2, 0, 1),
        (x_down_top, -1, 1, 0),
        (x_up_bottom, 1, 1, 1),
        (x_up_top, 1, 1, 0),
        (x_down_bottom, -1, 1, 1),
        (x_far_top, 2, 1, 0),
        (x_far_bottom, 2, 1, 1),
    ]


def on_device(start_panels, kinetic, fields):
    rank = start_panels.shape[1]
    rows, sites = kinetic.shape
    tm_size, inner_size = lax.axis_size("tm"), lax.axis_size("inner")
    hops = tm_size // 2
    inner = lax.axis_index("inner").astype(jnp.int32)
    z = lax.rem(lax.axis_index("tm").astype(jnp.int32), 2 * tm_size // X_CHIPS)
    y, xl, core = inner // (2 * CORES), inner // CORES % 2, inner % CORES
    sign = 1 - 2 * (z % 2)

    def pair_index(dy, dx):
        return (y + dy) % Y_CHIPS * 2 + (xl ^ dx)

    pairs = [
        ((t + i % hops) % tm_size * inner_size + i, t * inner_size + i)
        for t in range(tm_size)
        for i in range(inner_size)
    ]
    pieces = gather_kinetic(kinetic)
    scales = jnp.exp(coupling * fields.astype(F32)).reshape(sites // LANES, LANES)
    scales = lax.ppermute(scales, ("tm", "inner"), pairs)
    blocks = lax.all_gather(jnp.concatenate([start_panels[0], scales], 0), "inner", axis=0)
    spots = [
        (core * (inner_size // CORES) + pair_index(0, 0)) * LANES,
        core * (sites // CORES),
        (1 - core) * (sites // CORES),
    ]
    spots += [pair_index(dy * sign, dx) * rows + part * rows // 2 for _, dy, dx, part in pieces]
    spots = jnp.stack(spots)
    mapped, scales, high, low = run_load(hops, spots, blocks, [piece[0] for piece in pieces])
    inverse = None
    parts = []
    for hop in range(hops):
        other = other_core(mapped)
        gram, own, *state = run_map(hop, hops, spots, mapped, other, inverse, scales, high, low)
        out, inverse = run_factor(hop, sites, gram, own)
        if state:
            (mapped,) = state
        parts.append(from_behind(out, hop) if 0 < hop < hops - TOGETHER else out)
    final = parts[-1][:1, :1]
    for hop in range(hops - TOGETHER, hops):
        block = parts[hop] if hop == hops - 1 else parts[hop] + 0.0 * final
        parts[hop] = from_behind(block, hop)
    orbitals = jnp.stack([part[:rank] for part in parts], 0)[None]
    logs = jnp.stack([part[rank : rank + 2].reshape(-1)[:rank] for part in parts], 0)[None]
    return (orbitals, logs)


def solution(mesh):
    placed = (P("tm", None, "inner"), P("inner", None), P("tm", None))
    return jax.shard_map(
        on_device,
        mesh=mesh,
        in_specs=placed,
        out_specs=(P("tm", None, None, "inner"), P("tm", None, None)),
        check_vma=False,
    )
```

```python
import functools
import math

import jax
import jax.numpy as jnp
from jax import lax
from jax.experimental import pallas as pl
from jax.experimental.pallas import tpu as pltpu
from jax.sharding import PartitionSpec as P

coupling = 0.17725
F32 = jnp.float32
BF16 = jnp.bfloat16
LANES = 128
PIVOTS = 8
BLOCK = 32
CHUNK = 256
TOGETHER = 3


Y_CHIPS = 4
X_CHIPS = 4
CORES = 2


def device(tm_size, x, y, z, core):
    z_chips = 2 * tm_size // X_CHIPS
    x, y, z = x % X_CHIPS, y % Y_CHIPS, z % z_chips
    return (x // 2 * z_chips + z, (y * 2 + x % 2) * CORES + core % CORES)


def route(block, target):
    tm_size, inner_size = lax.axis_size("tm"), lax.axis_size("inner")
    pairs = []
    for x in range(X_CHIPS):
        for y in range(Y_CHIPS):
            for z in range(2 * tm_size // X_CHIPS):
                for core in range(CORES):
                    source = device(tm_size, x, y, z, core)
                    sink = device(tm_size, *target(x, y, z, core))
                    pairs.append(tuple(tm * inner_size + i for tm, i in (source, sink)))
    return lax.ppermute(block, ("tm", "inner"), pairs)


def along_x(block, by):
    return route(block, lambda x, y, z, core: (x + by, y, z, core))


def along_y(block, by):
    return route(block, lambda x, y, z, core: (x, y + by, z, core))


def along_y_by_parity(block, by):
    return route(block, lambda x, y, z, core: (x, y + (by if z % 2 == 0 else -by), z, core))


def along_z(block, by):
    return route(block, lambda x, y, z, core: (x, y, z + by, core))


def other_core(block):
    return route(block, lambda x, y, z, core: (x, y, z, core + 1))


def from_behind(block, distance):
    tm_size = lax.axis_size("tm")
    return lax.ppermute(block, "tm", [((i - distance) % tm_size, i) for i in range(tm_size)])


def halves(value):
    high = value.astype(BF16)
    return high, (value - high.astype(F32)).astype(BF16)


def last_with_last(left, right):
    return lax.dot_general(left, right, (((1,), (1,)), ((), ())), preferred_element_type=F32)


def last_with_first(left, right):
    return lax.dot_general(left, right, (((1,), (0,)), ((), ())), preferred_element_type=F32)


def factor(gram_ref, inverse_ref, pivot_ref):
    size = gram_ref.shape[0]
    lane = lax.broadcasted_iota(jnp.int32, (size, LANES), 1)
    row = lax.broadcasted_iota(jnp.int32, (size, LANES), 0)
    sublane = lax.broadcasted_iota(jnp.int32, (PIVOTS, LANES), 0)
    cut = size - LANES
    second = jnp.where(row - LANES == lane - cut, 1.0, 0.0)
    tiles = [
        gram_ref[:, :LANES],
        jnp.where(lane < cut, gram_ref[:, LANES:], second),
        jnp.where(row == lane, 1.0, 0.0),
    ]

    def columns_at(source, column):
        start = column % LANES
        return [
            jnp.broadcast_to(source[:, start + j : start + j + 1], (source.shape[0], LANES))
            for j in range(PIVOTS)
        ]

    for first in range(0, size, BLOCK):
        last = first + BLOCK
        live = [t for t in range(3) if t > 0 or first < LANES]
        part = {t: tiles[t][:BLOCK] for t in live}
        done = {t: [] for t in live}
        columns = columns_at(part[first // LANES], first)
        for top in range(0, BLOCK, PIVOTS):
            column = first + top
            ahead = []
            if top + PIVOTS < BLOCK:
                ahead = columns_at(part[(column + PIVOTS) // LANES], column + PIVOTS)
            pivots = jnp.zeros((PIVOTS, LANES), F32)
            for j in range(PIVOTS):
                pivots = jnp.where(sublane == j, columns[j][:PIVOTS], pivots)
                scaled = columns[j] * (1.0 / columns[j][j : j + 1, :])
                below = jnp.where(sublane > j, scaled[:PIVOTS], 0.0)
                if scaled.shape[0] > PIVOTS:
                    below = jnp.concatenate([below, scaled[PIVOTS:]], 0)
                for k in range(j + 1, PIVOTS):
                    columns[k] = columns[k] - below * columns[k][j : j + 1, :]
                ahead = [later - below * later[j : j + 1, :] for later in ahead]
                for t in live:
                    part[t] = part[t] - below * part[t][j : j + 1, :]
            columns = [later[PIVOTS:] for later in ahead]
            root = lax.rsqrt(pivots)
            root = root * (1.5 - 0.5 * pivots * root * root)
            pivot_ref[column : column + PIVOTS, :] = pivots
            for t in live:
                done[t].append(part[t][:PIVOTS] * root)
                part[t] = part[t][PIVOTS:]
        full = {t: jnp.concatenate(done[t], 0) for t in live}
        inverse_ref[first:last, :LANES] = full[2]
        padding = jnp.zeros((BLOCK, LANES - cut), F32)
        corner = full[1][:, cut:] if last > LANES else jnp.zeros((BLOCK, cut), F32)
        inverse_ref[first:last, LANES:] = jnp.concatenate([corner, padding], 1)
        if last == size:
            break
        if last < LANES:
            left = jnp.concatenate([full[0][:, last:], full[1][:, :cut]], 1)
        else:
            left = full[1][:, last - LANES : cut]
        live = [t for t in range(3) if t > 0 or last < LANES]
        left_high, left_low = halves(left)
        right_high, right_low = halves(jnp.concatenate([full[t] for t in live], 1))
        update = lax.dot_general(
            jnp.concatenate([left_high, left_high, left_low, left_low], 0),
            jnp.concatenate([right_high, right_low, right_high, right_low], 0),
            (((0,), (0,)), ((), ())),
            preferred_element_type=F32,
        )
        for i, t in enumerate(live):
            tiles[t] = tiles[t][BLOCK:] - update[:, LANES * i : LANES * i + LANES]
        if last >= LANES:
            tiles[0] = None


def map_chunk(panel, kinetic_high, kinetic_low, scale, c):
    rank = panel.shape[0] // 2
    at = slice(c * CHUNK, (c + 1) * CHUNK)
    both = last_with_last(panel[...], kinetic_high[at, :])
    rest = last_with_last(panel[:rank, :], kinetic_low[at, :])
    return (both[:rank] + both[rank:] + rest) * scale


def put(target, at, value):
    rank = target.shape[0] // 2
    high, low = halves(value)
    target[:rank, at] = high
    target[rank:, at] = low


def fill_gram(panel, gram_ref):
    rank = panel.shape[0] // 2
    both = panel[...]
    products = last_with_last(both, both)
    gram = (products[:rank, :rank] + products[rank:, rank:]) + (
        products[:rank, rank:] + products[rank:, :rank]
    )
    gram_ref[:, :LANES] = gram[:, :LANES]
    gram_ref[:, LANES:] = jnp.concatenate(
        [gram[:, LANES:], jnp.zeros((rank, 2 * LANES - rank), F32)], 1
    )


def factor_kernel(root, gram_ref, own_ref, out_ref, inverse_pair, inverse_ref, pivot_ref):
    rank = gram_ref.shape[0]
    factor(gram_ref, inverse_ref, pivot_ref)
    high, low = halves(inverse_ref[:, :rank])
    inverse_pair[:rank, :] = high
    inverse_pair[rank:, :] = low
    products = last_with_first(inverse_pair[...], own_ref[:rank])
    rest = last_with_first(inverse_pair[:rank, :], own_ref[rank:])
    diagonal = lax.broadcasted_iota(jnp.int32, (LANES, LANES), 0) == lax.broadcasted_iota(
        jnp.int32, (LANES, LANES), 1
    )
    lane = lax.broadcasted_iota(jnp.int32, (1, LANES), 1)
    upper = jnp.sum(jnp.where(diagonal, pivot_ref[:LANES], 0.0), 0, keepdims=True)
    under = jnp.where(diagonal[: rank - LANES], pivot_ref[LANES:], 0.0)
    under = jnp.where(lane < rank - LANES, jnp.sum(under, 0, keepdims=True), 1.0)
    out_ref[:rank, :] = (products[:rank] + products[rank:] + rest) * root
    out_ref[rank:, :] = jnp.concatenate(
        [0.5 * jnp.log(upper), 0.5 * jnp.log(under), jnp.zeros((6, LANES), F32)], 0
    )


def run_factor(hop, sites, gram, own):
    rank = gram.shape[0]
    vmem = pl.BlockSpec(memory_space=pltpu.VMEM)
    return pl.pallas_call(
        functools.partial(factor_kernel, math.sqrt(sites)),
        out_shape=(
            jax.ShapeDtypeStruct((rank + 8, LANES), F32),
            jax.ShapeDtypeStruct((2 * rank, rank), BF16),
        ),
        in_specs=[vmem, vmem],
        out_specs=(vmem, vmem),
        scratch_shapes=[
            pltpu.VMEM((rank, 2 * LANES), F32),
            pltpu.VMEM((rank, LANES), F32),
        ],
        compiler_params=pltpu.CompilerParams(vmem_limit_bytes=16 << 20),
        cost_estimate=pl.CostEstimate(
            flops=5 * rank * sites * sites, bytes_accessed=4 * rank * rank, transcendentals=0
        ),
        name="factor_" + str(hop),
    )(gram, own)


def spread(spots, core_spot, c, size):
    return pl.ds(pl.multiple_of(spots[core_spot] + c * size, size), size)


def load_kernel(pieces):
    def kernel(spots, blocks_in, *refs):
        kinetic = refs[:pieces]
        mapped, scale_ref, high_ref, low_ref, panel, blocks, own_rows, arrived = refs[pieces:]
        rank, tiles = panel.shape[0] // 2, panel.shape[1] // LANES
        hops = scale_ref.shape[0]
        lanes = [(r % CORES * (tiles // CORES) + r // CORES) * LANES for r in range(tiles)]
        copies = [
            pltpu.make_async_copy(kinetic[0], own_rows, arrived.at[0]),
            pltpu.make_async_copy(blocks_in, blocks, arrived.at[1]),
        ]
        for copy in copies:
            copy.start()
        for p in list(range(1, pieces)) + [0]:
            if p == 0:
                copies[0].wait()
            source = kinetic[p] if p else own_rows
            size = source.shape[0]
            at = pl.multiple_of(spots[3 + p], size)
            for r in range(tiles):
                high, low = halves(source[:, r * LANES : (r + 1) * LANES])
                high_ref[pl.ds(at, size), lanes[r] : lanes[r] + LANES] = high
                low_ref[pl.ds(at, size), lanes[r] : lanes[r] + LANES] = low
        copies[1].wait()
        for b in range(tiles):
            put(panel, slice(lanes[b], lanes[b] + LANES), blocks[b, :rank, :])
        for hop in range(hops):
            for r in range(tiles):
                scale_ref[hop, :, lanes[r] : lanes[r] + LANES] = blocks[
                    hop, rank + r : rank + r + 1, :
                ]
        for c in range(mapped.shape[1] // CHUNK):
            scale = scale_ref[0, :, spread(spots, 1, c, CHUNK)]
            mapped[:, c * CHUNK : (c + 1) * CHUNK] = map_chunk(panel, high_ref, low_ref, scale, c)

    return kernel


def run_load(hops, spots, blocks, kinetic):
    sites = kinetic[0].shape[1]
    rank = blocks.shape[1] - sites // LANES
    rows = sites // CORES
    vmem = pl.BlockSpec(memory_space=pltpu.VMEM)
    hbm = pl.BlockSpec(memory_space=pltpu.HBM)
    return pl.pallas_call(
        load_kernel(len(kinetic)),
        out_shape=(
            jax.ShapeDtypeStruct((rank, rows), F32),
            jax.ShapeDtypeStruct((hops, 1, sites), F32),
            jax.ShapeDtypeStruct((rows, sites), BF16),
            jax.ShapeDtypeStruct((rows, sites), BF16),
        ),
        in_specs=[pl.BlockSpec(memory_space=pltpu.SMEM), hbm, hbm]
        + [vmem] * (len(kinetic) - 1),
        out_specs=(vmem, vmem, vmem, vmem),
        scratch_shapes=[
            pltpu.VMEM((2 * rank, sites), BF16),
            pltpu.VMEM(blocks.shape, F32),
            pltpu.VMEM(kinetic[0].shape, F32),
            pltpu.SemaphoreType.DMA((2,)),
        ],
        compiler_params=pltpu.CompilerParams(vmem_limit_bytes=30 << 20),
        cost_estimate=pl.CostEstimate(
            flops=6 * rank * rows * sites, bytes_accessed=4 * rows * sites, transcendentals=0
        ),
        name="load",
    )(spots, blocks, *kinetic)


def map_kernel(hop, last):
    def kernel(spots, mine, other, *refs):
        if hop:
            inverse_in, refs = refs[0], refs[1:]
        if last:
            gram_ref, own_ref, panel = refs
        else:
            scale_ref, high_ref, low_ref, gram_ref, own_ref, mapped, panel = refs
        rank = panel.shape[0] // 2
        chunks = mine.shape[1] // CHUNK
        for c in range(chunks):
            at = slice(c * CHUNK, (c + 1) * CHUNK)
            for half, source in ((1, mine), (2, other)):
                value = source[:, at]
                if hop:
                    high, low = halves(value)
                    products = last_with_first(inverse_in[...], high)
                    rest = last_with_first(inverse_in[:rank, :], low)
                    value = products[:rank] + products[rank:] + rest
                put(panel, spread(spots, half, c, CHUNK), value)
        own_ref[...] = panel[:, pl.ds(pl.multiple_of(spots[0], LANES), LANES)]
        fill_gram(panel, gram_ref)
        if not last:
            for c in range(chunks):
                scale = scale_ref[hop + 1, :, spread(spots, 1, c, CHUNK)]
                value = map_chunk(panel, high_ref, low_ref, scale, c)
                mapped[:, c * CHUNK : (c + 1) * CHUNK] = value

    return kernel


def run_map(hop, hops, spots, mine, other, inverse, scales, high, low):
    rank, rows = mine.shape
    sites = rows * CORES
    last = hop == hops - 1
    vmem = pl.BlockSpec(memory_space=pltpu.VMEM)
    operands = [inverse] if hop else []
    operands += [] if last else [scales, high, low]
    shapes = [
        jax.ShapeDtypeStruct((rank, 2 * LANES), F32),
        jax.ShapeDtypeStruct((2 * rank, LANES), BF16),
    ]
    if not last:
        shapes += [jax.ShapeDtypeStruct((rank, rows), F32)]
    return pl.pallas_call(
        map_kernel(hop, last),
        out_shape=shapes,
        in_specs=[pl.BlockSpec(memory_space=pltpu.SMEM), vmem, vmem] + [vmem] * len(operands),
        out_specs=[vmem] * len(shapes),
        scratch_shapes=[pltpu.VMEM((2 * rank, sites), BF16)],
        compiler_params=pltpu.CompilerParams(vmem_limit_bytes=24 << 20),
        cost_estimate=pl.CostEstimate(
            flops=6 * rank * rows * sites, bytes_accessed=4 * rank * sites, transcendentals=0
        ),
        name="map_" + str(hop),
    )(spots, mine, other, *operands)


def gather_kinetic(kinetic):
    half = kinetic.shape[0] // 2
    top, bottom = kinetic[:half], kinetic[half:]
    down, up = along_y_by_parity(top, 1), along_y_by_parity(bottom, -1)
    across, back = along_x(top, 1), along_x(bottom, -1)
    far_top, far_bottom = along_y_by_parity(down, 1), along_y_by_parity(up, -1)
    x_down_top, x_up_bottom = along_x(down, 1), along_x(up, -1)
    up_top, down_bottom = along_z(down, 1), along_z(up, -1)
    x_far_top, x_far_bottom = along_x(far_top, 1), along_x(far_bottom, -1)
    x_up_top, x_down_bottom = along_z(x_down_top, 1), along_z(x_up_bottom, -1)
    return [
        (kinetic, 0, 0, 0),
        (down, -1, 0, 0),
        (up, 1, 0, 1),
        (across, 0, 1, 0),
        (back, 0, 1, 1),
        (up_top, 1, 0, 0),
        (down_bottom, -1, 0, 1),
        (far_top, 2, 0, 0),
        (far_bottom, 2, 0, 1),
        (x_down_top, -1, 1, 0),
        (x_up_bottom, 1, 1, 1),
        (x_up_top, 1, 1, 0),
        (x_down_bottom, -1, 1, 1),
        (x_far_top, 2, 1, 0),
        (x_far_bottom, 2, 1, 1),
    ]


def on_device(start_panels, kinetic, fields):
    rank = start_panels.shape[1]
    rows, sites = kinetic.shape
    tm_size, inner_size = lax.axis_size("tm"), lax.axis_size("inner")
    hops = tm_size // 2
    inner = lax.axis_index("inner").astype(jnp.int32)
    z = lax.rem(lax.axis_index("tm").astype(jnp.int32), 2 * tm_size // X_CHIPS)
    y, xl, core = inner // (2 * CORES), inner // CORES % 2, inner % CORES
    sign = 1 - 2 * (z % 2)

    def pair_index(dy, dx):
        return (y + dy) % Y_CHIPS * 2 + (xl ^ dx)

    pairs = [
        ((t + i % hops) % tm_size * inner_size + i, t * inner_size + i)
        for t in range(tm_size)
        for i in range(inner_size)
    ]
    pieces = gather_kinetic(kinetic)
    scales = jnp.exp(coupling * fields.astype(F32)).reshape(sites // LANES, LANES)
    scales = lax.ppermute(scales, ("tm", "inner"), pairs)
    blocks = lax.all_gather(jnp.concatenate([start_panels[0], scales], 0), "inner", axis=0)
    spots = [
        (core * (inner_size // CORES) + pair_index(0, 0)) * LANES,
        core * (sites // CORES),
        (1 - core) * (sites // CORES),
    ]
    spots += [pair_index(dy * sign, dx) * rows + part * rows // 2 for _, dy, dx, part in pieces]
    spots = jnp.stack(spots)
    mapped, scales, high, low = run_load(hops, spots, blocks, [piece[0] for piece in pieces])
    inverse = None
    parts = []
    for hop in range(hops):
        other = other_core(mapped)
        gram, own, *state = run_map(hop, hops, spots, mapped, other, inverse, scales, high, low)
        out, inverse = run_factor(hop, sites, gram, own)
        if state:
            (mapped,) = state
        parts.append(from_behind(out, hop) if 0 < hop < hops - TOGETHER else out)
    final = parts[-1][:1, :1]
    for hop in range(hops - TOGETHER, hops):
        block = parts[hop] if hop == hops - 1 else parts[hop] + 0.0 * final
        parts[hop] = from_behind(block, hop)
    orbitals = jnp.stack([part[:rank] for part in parts], 0)[None]
    logs = jnp.stack([part[rank : rank + 2].reshape(-1)[:rank] for part in parts], 0)[None]
    return (orbitals, logs)


def solution(mesh):
    placed = (P("tm", None, "inner"), P("inner", None), P("tm", None))
    return jax.shard_map(
        on_device,
        mesh=mesh,
        in_specs=placed,
        out_specs=(P("tm", None, None, "inner"), P("tm", None, None)),
        check_vma=False,
    )
```
